512 devices in a mesh: grp: 16 (over z, core), ep: 32 (over x, y).
Axes of the slice: x: 4, y: 8, z: 8, core: 2. Of those that a mesh axis runs over, the one named last changes fastest.
Arguments:
- q_raw: bfloat16 [8192, 4096], P(('grp', 'ep')), may hold values from -6 to 6
- k_raw: bfloat16 [8192, 512], P(('grp', 'ep')), may hold values from -6 to 6
- v_raw: bfloat16 [8192, 512], P(('grp', 'ep')), may hold values from -6 to 6
- q_gain: float32 [128], replicated, may hold values from 0.5 to 1.5
- k_gain: float32 [128], replicated, may hold values from 0.5 to 1.5
- caches: bfloat16 [16, 1024, 2, 2, 512], P('grp', 'ep'), may hold values from -4 to 4
- lengths: int32 [16, 32], P('grp', 'ep'), may hold values from 1 to 16, 448 in all within a row
- cont_owner: int32 [16, 32], P('grp', 'ep'), may hold values from 0 to 31, as said below
- out_weight: bfloat16 [4096, 2048], P(None, 'grp'), may hold values from -1 to 1
- residual: bfloat16 [8192, 2048], P(('grp', 'ep')), may hold values from -24 to 24
- moe_gain: float32 [2048], replicated, may hold values from 0.1 to 1.9
- routes: int32 [8192, 8], P(('grp', 'ep')), may hold values from 0 to 127, all different within a row; in each aligned block of 16 rows (0 to 15, 16 to 31, ...) at most 2 rows name the same one
- gate_weights: float32 [8192, 8], P(('grp', 'ep')), may hold values from 0.05 to 0.3
- w_in: bfloat16 [2, 2048, 98304], P(None, None, ('grp', 'ep')), may hold values from -0.125 to 0.125
- w_down: bfloat16 [98304, 2048], P(('grp', 'ep')), may hold values from -0.21875 to 0.21875
Outputs:
- mixed: bfloat16 [8192, 2048], P(('grp', 'ep'))
The draws below stay inside these ranges and needn't reach their ends.
Inputs may be any that keep to these rules, and one draw needn't show every extreme that they name: `routes`: in the rows of one device (aligned blocks of 16 rows) no expert is named by more than 2 rows, a bound that some block reaches. The 32 lengths of a group sum to 448 and the longest is 16. `cont_owner`: entry [g, p] names a device of group g; for some requests it is p itself.
All inputs are finite; a program needn't handle non-finite values.
Results may differ from the reference program's by a relative error of at most 0.0065.
The reference program's roundings to bfloat16 on the way count: a program that leaves them out, or rounds other values in their place, can miss the bound.
Values may be sent and summed in bfloat16 or wider, within the bound.
A program may use at most 64 MiB of HBM per device.

```python
import math
import jax
import jax.numpy as jnp
import numpy as np
from jax import lax

D = 2048
HEADS = 32
KV_HEADS = 4
HD = 128
FF = 768
TOP = 8
SPLIT = 4
TOK_DEV = 16
KV_DEV = 32
GROUPS = 16
COLUMNS = 32
EXPERTS = 128
EXP_FF = 192
PREFIX = 1024
TOKENS = 8192
CAP = 2
DEVICES = 512


def draw_cont_owner(key, part):
    first_key, second_key = jax.random.split(key)
    elsewhere = jax.random.randint(first_key, (GROUPS, COLUMNS), 0, COLUMNS)
    moved = jax.random.randint(second_key, (GROUPS, COLUMNS), 0, 2)
    itself = jnp.broadcast_to(jnp.arange(COLUMNS, dtype=jnp.int32)[None, :], (GROUPS, COLUMNS))
    return jnp.where(moved == 1, elsewhere, itself).astype(jnp.int32)


def draw_residual(key, part):
    base_key, column_key, row_key = jax.random.split(key, 3)
    base = jnp.clip(jax.random.normal(base_key, (TOKENS, D), jnp.float32), -4.0, 4.0)
    column_scale = jnp.exp(jax.random.uniform(column_key, (D,), jnp.float32, math.log(0.3), math.log(3.0)))
    row_scale = jnp.exp(jax.random.uniform(row_key, (TOKENS, 1), jnp.float32, math.log(0.5), math.log(2.0)))
    return (base * column_scale[None, :] * row_scale).astype(jnp.bfloat16)


def block_scale(rng, extent, cuts, least, high):
    gain = 1.0
    for axis_at, blocks in cuts:
        draws = jax.random.uniform(jax.random.fold_in(jax.random.fold_in(rng, 6), axis_at), (blocks,), jnp.float32, least / len(cuts), high / len(cuts))
        gain = gain * jnp.repeat(jnp.exp(draws), extent[axis_at] // blocks).reshape((-1,) + (1,) * (len(extent) - 1 - axis_at))
    return gain


def length_profile(count, total, limit, slope):
    loads = [(1 << 20) // math.isqrt(standing ** slope) + 1 for standing in range(2, count + 1)]
    surplus, holding = total - limit - (count - 1), [1] * (count - 1)
    while surplus > 0:
        movable = [i for i in range(count - 1) if holding[i] < limit]
        mass, left = sum([loads[i] for i in movable]), surplus
        for i in movable:
            addition = min(limit - holding[i], max(1, left * loads[i] // mass), surplus)
            holding[i] = holding[i] + addition
            surplus = surplus - addition
    return np.array([limit] + holding)


def ragged_sizes(stream_key, number_of, total, most, slope):
    if number_of == 2:
        one = jax.random.randint(stream_key, (), max(1, total - most), min(most, total - 1) + 1)
        return jnp.stack([one, total - one])
    sizes = jnp.asarray(length_profile(number_of, total, most, slope), jnp.int32)
    pairs = (number_of - 1) // 2
    donor, sink = sizes[1:1 + 2 * pairs:2], sizes[2:2 + 2 * pairs:2]
    margin = jnp.minimum(donor - 1, most - sink)
    passed = jax.random.randint(jax.random.fold_in(stream_key, 1), (pairs,), 0, 1 << 20) % (margin + 1)
    sizes = sizes.at[1:1 + 2 * pairs:2].set(donor - passed).at[2:2 + 2 * pairs:2].set(sink + passed)
    return sizes[jax.random.permutation(jax.random.fold_in(stream_key, 2), number_of)]


def routed_block(own_key, own, number, rows, amount, top, bound, slope):
    order = jax.random.permutation(own_key, amount)
    heavy_load, common = shares(amount, rows * top, bound, slope, True), shares(amount, rows * top, bound, slope, False)
    places = jnp.arange(amount)

    def named(sizes, rotation):
        used = int((sizes > 0).sum())
        fixed = max(1, used // 4)
        passed = fixed + (places - fixed + rotation * (used - fixed)) % max(1, amount - fixed)
        return jnp.zeros((amount,), jnp.int32).at[order[jnp.where(places < fixed, places, passed)]].set(jnp.asarray(sizes, jnp.int32))

    sizes = jnp.where(number % 4 == 0, named(heavy_load, number // 4), named(common, number - number // 4 - 1))
    mixed = jax.random.permutation(jax.random.fold_in(own, 3), amount)
    giver, taker = mixed[0:amount // 2 * 2:2], mixed[1:amount // 2 * 2:2]
    room = jnp.minimum(sizes[giver] - 1, bound - sizes[taker]) // 2
    room = jnp.where((giver == order[0]) | (taker == order[0]) | (sizes[taker] == 0), 0, jnp.maximum(room, 0))
    passed = jax.random.randint(jax.random.fold_in(own, 4), (amount // 2,), 0, 1 << 20) % (room + 1)
    sizes = sizes.at[giver].add(-passed).at[taker].add(passed)
    labels = jnp.searchsorted(jnp.cumsum(sizes), jnp.arange(rows * top), side="right").astype(jnp.int32)
    table = labels.reshape(top, rows).T
    table = table[jax.random.permutation(jax.random.fold_in(own, 1), rows)]
    rotation = jax.random.randint(jax.random.fold_in(own, 2), (rows, 1), 0, top)
    return jnp.take_along_axis(table, (jnp.arange(top)[None, :] + rotation) % top, axis=1)


def shares(number_of, total, limit, slope, full):
    portions = [(1 << 20) // math.isqrt(standing ** slope) + 1 for standing in range(1, number_of + 1)]
    largest = limit if full else min(limit, max(-(-total // number_of), total * portions[0] // sum(portions)))
    least = 1 if total - largest >= number_of - 1 else 0
    given, surplus = [largest] + [least] * (number_of - 1), total - largest - least * (number_of - 1)
    while surplus > 0:
        movable = [i for i in range(1, number_of) if given[i] < largest] or [i for i in range(1, number_of) if given[i] < limit]
        whole, remaining = sum([portions[i] for i in movable]), surplus
        for i in movable:
            more = min(limit - given[i], max(1, remaining * portions[i] // whole), surplus)
            given[i] = given[i] + more
            surplus = surplus - more
    return np.array(given)


def scatter_about(key, dims, spread, bound, shards=(), kind=jnp.bfloat16):
    drawn = jax.random.normal(key, dims, jnp.float32) * spread
    if len(shards) > 0:
        drawn = block_scale(key, dims, shards, -0.22, 0.18) * drawn
    return jnp.clip(drawn, min=-bound, max=bound).astype(kind)


def setup_inputs(seed: int = 0) -> dict:
    splits = jax.random.split(jax.random.key(seed), 16)
    q_raw = scatter_about(splits[0], (TOKENS, HEADS * HD), 1.0, 6.0, ((0, 512),))
    k_raw = scatter_about(splits[1], (TOKENS, KV_HEADS * HD), 1.0, 6.0, ((0, 512),))
    v_raw = scatter_about(splits[2], (TOKENS, KV_HEADS * HD), 2.0, 6.0, ((0, 512),))
    q_gain = jnp.clip(1.0 + 0.1 * jax.random.normal(splits[3], (HD,), jnp.float32), 0.5, 1.5)
    k_gain = jnp.clip(1.0 + 0.1 * jax.random.normal(splits[4], (HD,), jnp.float32), 0.5, 1.5)
    caches = scatter_about(splits[5], (GROUPS, COLUMNS * KV_DEV, 2, 2, KV_HEADS * HD), 1.0, 4.0, ((0, 16), (1, 32)))
    lengths = jax.vmap(lambda own: ragged_sizes(own, COLUMNS, COLUMNS * TOK_DEV * 7 // 8, TOK_DEV, 2))(jax.random.split(splits[6], GROUPS)).reshape((GROUPS, COLUMNS)).astype(jnp.int32)
    cont_owner = draw_cont_owner(jax.random.fold_in(splits[15], 71), 0)
    out_weight = scatter_about(splits[8], (HEADS * HD, D), (HD // 4) ** -0.5, 1.0, ((1, 16),))
    residual = draw_residual(jax.random.fold_in(splits[15], 71), 0)
    moe_gain = jnp.clip(1.0 + 0.18 * jax.random.normal(splits[10], (D,), jnp.float32), 0.1, 1.9)
    routes_keys = jax.random.split(jax.random.fold_in(splits[11], 1), TOKENS // TOK_DEV)
    routes_turns = jax.random.permutation(jax.random.fold_in(splits[11], 3), TOKENS // TOK_DEV)
    routes = jax.vmap(lambda own, number: routed_block(jax.random.fold_in(splits[11], 2), own, number, TOK_DEV, EXPERTS, TOP, CAP, 2))(routes_keys, routes_turns).reshape((TOKENS, TOP))
    gate_weights = jnp.clip(0.05 + 0.25 * jax.random.uniform(splits[12], (TOKENS, TOP), jnp.float32) ** block_scale(splits[12], (TOKENS, TOP), ((0, 512),), -0.2, 0.2), 0.05, 0.3)
    w_in = scatter_about(splits[13], (2, D, EXPERTS * FF), D ** -0.5, 0.125, ((2, 512),))
    w_down = scatter_about(splits[14], (EXPERTS * FF, D), FF ** -0.5, 0.21875, ((0, 512),))
    return dict(q_raw=q_raw, k_raw=k_raw, v_raw=v_raw, q_gain=q_gain, k_gain=k_gain, caches=caches, lengths=lengths, cont_owner=cont_owner, out_weight=out_weight, residual=residual, moe_gain=moe_gain, routes=routes, gate_weights=gate_weights, w_in=w_in, w_down=w_down)


theta_base = 1000000.0
eps_norm = 1e-06

def normed(values, scales):
    return values * lax.rsqrt(lax.optimization_barrier(jnp.mean(values * values, axis=-1, keepdims=True)) + eps_norm) * scales

def rotate(values, position):
    head_width = values.shape[-1]
    half_width = head_width // 2
    inv_freq = jnp.power(theta_base, -2.0 * jnp.arange(half_width, dtype=jnp.float32) / head_width)
    angles = position[:, None] * inv_freq[None, :]
    cosine = jnp.cos(angles)[:, None, :]
    sine_part = jnp.sin(angles)[:, None, :]
    first_half = values[..., :half_width]
    second_half = values[..., half_width:]
    return jnp.concatenate([first_half * cosine - second_half * sine_part, second_half * cosine + first_half * sine_part], axis=-1)

def rounded(values):
    return lax.optimization_barrier(values.astype(jnp.bfloat16)).astype(jnp.float32)

def reference(q_raw, k_raw, v_raw, q_gain, k_gain, caches, lengths, cont_owner, out_weight, residual, moe_gain, routes, gate_weights, w_in, w_down):
    group_size = HEADS // KV_HEADS
    slot_idx = jnp.arange(TOK_DEV, dtype=jnp.int32)
    position = (PREFIX + KV_DEV + slot_idx).astype(jnp.float32)
    queries = normed(q_raw.astype(jnp.float32).reshape(DEVICES, TOK_DEV, HEADS, HD), q_gain)
    queries = rotate(queries, position).astype(jnp.bfloat16).reshape(GROUPS, COLUMNS, TOK_DEV, KV_HEADS, group_size, HD)
    new_keys = normed(k_raw.astype(jnp.float32).reshape(DEVICES, TOK_DEV, KV_HEADS, HD), k_gain)
    new_keys = rotate(new_keys, position).astype(jnp.bfloat16).reshape(GROUPS, COLUMNS, TOK_DEV, KV_HEADS, HD)
    new_values = v_raw.reshape(GROUPS, COLUMNS, TOK_DEV, KV_HEADS, HD)
    stored = caches.reshape(GROUPS, COLUMNS, KV_DEV, 2, 2, KV_HEADS, HD)
    scaling = 1.0 / math.sqrt(HD)

    def one_group(inputs):
        group_query, keys_new, values_new, cached, seq_lens, owner_col = inputs
        query_f = group_query.astype(jnp.float32)
        pre_keys = cached[:, :, 0, 0].reshape(COLUMNS * KV_DEV, KV_HEADS, HD).astype(jnp.float32)
        pre_values = cached[:, :, 0, 1].reshape(COLUMNS * KV_DEV, KV_HEADS, HD).astype(jnp.float32)
        pre_weights = jnp.exp(jnp.einsum('ctkgd,nkd->ctkgn', query_f, pre_keys) * scaling)
        numerator = jnp.einsum('ctkgn,nkd->ctkgd', rounded(pre_weights), pre_values)
        denominator = lax.optimization_barrier(jnp.sum(pre_weights, axis=-1))
        cont_rows = jnp.take(cached, owner_col, axis=0)
        cont_keys = cont_rows[:, :, 1, 0].astype(jnp.float32)
        cont_values = cont_rows[:, :, 1, 1].astype(jnp.float32)
        cont_weights = jnp.exp(jnp.einsum('ctkgd,cnkd->ctkgn', query_f, cont_keys) * scaling)
        numerator = numerator + jnp.einsum('ctkgn,cnkd->ctkgd', rounded(cont_weights), cont_values)
        denominator = denominator + lax.optimization_barrier(jnp.sum(cont_weights, axis=-1))
        own_scores = jnp.einsum('ctkgd,cskd->ctkgs', query_f, keys_new.astype(jnp.float32)) * scaling
        causal_mask = (slot_idx[None, None, :] <= slot_idx[None, :, None]) & (slot_idx[None, None, :] < seq_lens[:, None, None])
        own_weights = jnp.where(causal_mask[:, :, None, None, :], jnp.exp(own_scores), 0.0)
        numerator = numerator + jnp.einsum('ctkgs,cskd->ctkgd', rounded(own_weights), values_new.astype(jnp.float32))
        denominator = denominator + lax.optimization_barrier(jnp.sum(own_weights, axis=-1))
        live_rows = slot_idx[None, :] < seq_lens[:, None]
        attn_rows = jnp.where(live_rows[:, :, None, None, None], numerator / denominator[..., None], 0.0)
        return attn_rows.astype(jnp.bfloat16).reshape(COLUMNS, TOK_DEV, HEADS * HD)
    attended = lax.map(one_group, (queries, new_keys, new_values, stored, lengths, cont_owner)).reshape(TOKENS, HEADS * HD)
    attn_proj = jnp.dot(attended, out_weight, preferred_element_type=jnp.float32).astype(jnp.bfloat16)
    hidden_state = (residual.astype(jnp.float32) + attn_proj.astype(jnp.float32)).astype(jnp.bfloat16)
    moe_in = normed(hidden_state.astype(jnp.float32), moe_gain).astype(jnp.bfloat16)
    live_slots = slot_idx[None, :] < lengths.reshape(DEVICES, 1)
    route_grid = jnp.where(live_slots[:, :, None], routes.reshape(DEVICES, TOK_DEV, TOP), -1)
    flat_route = route_grid.reshape(DEVICES, TOK_DEV * TOP)
    assign_idx = jnp.arange(TOK_DEV * TOP, dtype=jnp.int32)
    earlier = assign_idx[None, :] < assign_idx[:, None]
    same_expert = flat_route[:, :, None] == flat_route[:, None, :]
    slot_rank = lax.optimization_barrier(jnp.sum((same_expert & earlier[None]).astype(jnp.int32), axis=2))
    cap_idx = jnp.arange(CAP, dtype=jnp.int32)
    slot_hot = (slot_rank[:, :, None] == cap_idx[None, None, :]).reshape(DEVICES, TOK_DEV, TOP, CAP)
    gate_grid = gate_weights.reshape(DEVICES, TOK_DEV, TOP)
    input_grid = moe_in.reshape(DEVICES, TOK_DEV, D).astype(jnp.float32)

    def expert_step(running, expert):
        matched = (route_grid == expert)[..., None] & slot_hot
        chosen = lax.optimization_barrier(jnp.sum(matched.astype(jnp.float32), axis=2))
        weighted = lax.optimization_barrier(jnp.sum(jnp.where(matched, gate_grid[..., None], 0.0), axis=2))
        gathered = jnp.einsum('ntc,ntf->ncf', chosen, input_grid).astype(jnp.bfloat16).reshape(DEVICES * CAP, D)
        out_sum = jnp.zeros((DEVICES * CAP, D), jnp.float32)
        for quarter_idx in range(SPLIT):
            first_unit = (expert * FF + quarter_idx * EXP_FF).astype(jnp.int32)
            gate_cols = lax.dynamic_slice_in_dim(w_in[0], first_unit, EXP_FF, axis=1)
            up_cols = lax.dynamic_slice_in_dim(w_in[1], first_unit, EXP_FF, axis=1)
            down_rows = lax.dynamic_slice_in_dim(w_down, first_unit, EXP_FF, axis=0)
            gate_act = jnp.dot(gathered, gate_cols, preferred_element_type=jnp.float32)
            up_act = jnp.dot(gathered, up_cols, preferred_element_type=jnp.float32)
            inner_act = (jax.nn.silu(gate_act) * up_act).astype(jnp.bfloat16)
            out_sum = out_sum + rounded(jnp.dot(inner_act, down_rows, preferred_element_type=jnp.float32))
        expert_out = rounded(out_sum)
        running = running + jnp.einsum('ntc,ncf->ntf', weighted, expert_out.reshape(DEVICES, CAP, D), precision=lax.Precision.HIGHEST)
        return (running, None)
    moe_out, _ = lax.scan(expert_step, jnp.zeros((DEVICES, TOK_DEV, D), jnp.float32), jnp.arange(EXPERTS, dtype=jnp.int32))
    result = jnp.where(live_slots[:, :, None], hidden_state.reshape(DEVICES, TOK_DEV, D).astype(jnp.float32) + moe_out, 0.0)
    return result.reshape(TOKENS, D).astype(jnp.bfloat16)
```

```python
import functools
import math

import jax
import jax.numpy as jnp
from jax import lax
from jax.experimental import pallas as pl
from jax.experimental.pallas import tpu as pltpu
from jax.sharding import PartitionSpec as P

theta_base = 1000000.0
eps_norm = 1e-06
f32 = jnp.float32
bf16 = jnp.bfloat16


def normed(values, scales):
    return values * lax.rsqrt(jnp.mean(values * values, axis=-1, keepdims=True) + eps_norm) * scales


def rotation_tables(position, head_width):
    half_width = head_width // 2
    inv_freq = jnp.power(theta_base, -2.0 * jnp.arange(half_width, dtype=f32) / head_width)
    angles = position[:, None] * inv_freq[None, :]
    cosine, sine = jnp.cos(angles), jnp.sin(angles)
    return jnp.concatenate([cosine, cosine], -1), jnp.concatenate([-sine, sine], -1)


def attention_body(
    kv_heads, cache_rows, len_ref, own_ref, q_ref, k_ref, v_ref, qg_ref, kg_ref, cos_ref, sin_ref, kv_ref, out_ref
):
    tok_count = q_ref.shape[0]
    hd = qg_ref.shape[1]
    width = kv_heads * hd
    group = q_ref.shape[1] // width
    rows = group * tok_count
    scaling = 1.0 / math.sqrt(hd)
    seq_len = len_ref[0, 0]
    start = pl.multiple_of(own_ref[0, 0] * cache_rows, cache_rows)
    cosine, sine = cos_ref[...], sin_ref[...]

    def prepared(raw, gain):
        values = normed(raw.astype(f32), gain)
        return (values * cosine + pltpu.roll(values, hd // 2, 1) * sine).astype(bf16)

    slot = lax.broadcasted_iota(jnp.int32, (rows, tok_count), 0) % tok_count
    other = lax.broadcasted_iota(jnp.int32, (rows, tok_count), 1)
    causal = (other <= slot) & (other < seq_len)
    live = lax.broadcasted_iota(jnp.int32, (rows, hd), 0) % tok_count < seq_len
    contract = (((1,), (1,)), ((), ()))

    def weighed(queries, keys):
        return jnp.exp(lax.dot_general(queries, keys, contract, preferred_element_type=f32) * scaling)

    for h in range(kv_heads):
        span = pl.ds(h * hd, hd)
        queries = jnp.concatenate(
            [prepared(q_ref[:, pl.ds((h * group + j) * hd, hd)], qg_ref[...]) for j in range(group)], 0
        )
        pre = weighed(queries, kv_ref[:, span])
        cont = weighed(queries, kv_ref[pl.ds(start, cache_rows), pl.ds(2 * width + h * hd, hd)])
        own = jnp.where(causal, weighed(queries, prepared(k_ref[:, span], kg_ref[...])), 0.0)
        numerator = (
            jnp.dot(pre.astype(bf16), kv_ref[:, pl.ds(width + h * hd, hd)], preferred_element_type=f32)
            + jnp.dot(
                cont.astype(bf16),
                kv_ref[pl.ds(start, cache_rows), pl.ds(3 * width + h * hd, hd)],
                preferred_element_type=f32,
            )
            + jnp.dot(own.astype(bf16), v_ref[:, span], preferred_element_type=f32)
        )
        denominator = (
            jnp.sum(pre, 1, keepdims=True) + jnp.sum(cont, 1, keepdims=True) + jnp.sum(own, 1, keepdims=True)
        )
        result = jnp.where(live, numerator / denominator, 0.0).astype(bf16)
        for j in range(group):
            out_ref[:, pl.ds((h * group + j) * hd, hd)] = result[j * tok_count : (j + 1) * tok_count]


def attention(q_raw, k_raw, v_raw, q_gain, k_gain, kv_block, lengths, cont_owner, cache_rows):
    hd = q_gain.shape[0]
    tok_count = q_raw.shape[0]
    position = (kv_block.shape[0] + cache_rows + jnp.arange(tok_count, dtype=jnp.int32)).astype(f32)
    cosine, sine = rotation_tables(position, hd)
    vmem = pl.BlockSpec(memory_space=pltpu.VMEM)
    smem = pl.BlockSpec(memory_space=pltpu.SMEM)
    return pl.pallas_call(
        functools.partial(attention_body, k_raw.shape[1] // hd, cache_rows),
        out_shape=jax.ShapeDtypeStruct(q_raw.shape, bf16),
        in_specs=[smem, smem] + [vmem] * 8,
        out_specs=vmem,
    )(lengths, cont_owner, q_raw, k_raw, v_raw, q_gain[None], k_gain[None], cosine, sine, kv_block)


def per_device(
    q_raw,
    k_raw,
    v_raw,
    q_gain,
    k_gain,
    caches,
    lengths,
    cont_owner,
    out_weight,
    residual,
    moe_gain,
    routes,
    gate_weights,
    w_in,
    w_down,
):
    n_groups = lax.axis_size("grp")
    n_columns = lax.axis_size("ep")
    tok_count, model_width = residual.shape
    cache_rows = caches.shape[1]
    top_count = routes.shape[1]
    pieces = 4
    expert_count = n_groups * n_columns // pieces
    local = expert_count // n_groups
    capacity = 2
    per_source = n_groups * capacity
    live_rows = jnp.arange(tok_count, dtype=jnp.int32) < lengths[0, 0]

    flat_route = jnp.where(live_rows[:, None], routes, -1).reshape(-1)
    assign_idx = jnp.arange(flat_route.shape[0], dtype=jnp.int32)
    matches = (flat_route[:, None] == flat_route[None, :]) & (assign_idx[None, :] < assign_idx[:, None])
    slot_rank = jnp.sum(matches.astype(jnp.int32), axis=1)
    place = jnp.where(flat_route >= 0, flat_route * capacity + slot_rank, -1)
    slots = jnp.arange(expert_count * capacity, dtype=jnp.int32)
    placed = place.reshape(tok_count, top_count, 1) == slots
    weighted = jnp.sum(jnp.where(placed, gate_weights[:, :, None], 0.0), axis=1)
    chosen = jnp.any(placed, axis=1)
    holder = jnp.sum(
        jnp.where(chosen, jnp.arange(1, tok_count + 1, dtype=jnp.int32)[:, None], 0), axis=0
    ) - 1
    holders = lax.all_gather(holder, "grp", axis=0, tiled=False)
    first = lax.axis_index("grp") * (local * capacity)
    mine = lax.dynamic_slice(holders, (0, first), (n_groups, local * capacity))
    wanted = mine.reshape(n_groups, local, capacity).transpose(1, 0, 2).reshape(-1)
    wanted = wanted.reshape(local, 1, per_source)
    source_row = jnp.arange(per_source, dtype=jnp.int32) // capacity * tok_count
    wanted = jnp.where(wanted >= 0, wanted + source_row, -1)
    wanted = jnp.broadcast_to(wanted, (local, pieces, per_source)).reshape(-1)
    select = (wanted[:, None] == jnp.arange(n_groups * tok_count, dtype=jnp.int32)[None, :]).astype(bf16)

    kv_block = lax.all_gather(caches.reshape(cache_rows, -1), "ep", axis=0, tiled=True)
    attended = attention(q_raw, k_raw, v_raw, q_gain, k_gain, kv_block, lengths, cont_owner, cache_rows)
    projected = jnp.dot(
        lax.all_gather(attended, "grp", axis=0, tiled=True), out_weight, preferred_element_type=f32
    ).astype(bf16)
    attn_proj = lax.all_to_all(projected, "grp", split_axis=0, concat_axis=1, tiled=True)
    hidden_state = (residual.astype(f32) + attn_proj.astype(f32)).astype(bf16)
    moe_in = normed(hidden_state.astype(f32), moe_gain).astype(bf16)

    tokens = lax.all_gather(moe_in, "grp", axis=0, tiled=True)
    outgoing = jnp.dot(select, tokens, preferred_element_type=f32).astype(bf16)
    received = lax.all_to_all(
        outgoing.reshape(n_columns, per_source, model_width), "ep", split_axis=0, concat_axis=0, tiled=True
    )
    rows_in = received.reshape(-1, model_width)
    gate_act = jnp.dot(rows_in, w_in[0], preferred_element_type=f32)
    up_act = jnp.dot(rows_in, w_in[1], preferred_element_type=f32)
    inner_act = (jax.nn.silu(gate_act) * up_act).astype(bf16)
    partial_out = jnp.dot(inner_act, w_down, preferred_element_type=f32).astype(bf16)
    returned = lax.all_to_all(
        partial_out.reshape(n_columns, per_source, model_width), "ep", split_axis=0, concat_axis=0, tiled=True
    ).reshape(-1, model_width)
    in_row = jnp.arange(n_columns * per_source, dtype=jnp.int32)
    in_slot = in_row % per_source
    target = (
        in_slot // capacity * (local * capacity)
        + in_row // (pieces * per_source) * capacity
        + in_slot % capacity
    )
    out_row = jnp.arange(n_groups * local * capacity, dtype=jnp.int32)
    gather_sum = (out_row[:, None] == target[None, :]).astype(bf16)
    summed = jnp.dot(gather_sum, returned, preferred_element_type=f32).astype(bf16)
    expert_out = lax.all_to_all(summed, "grp", split_axis=0, concat_axis=0, tiled=True)
    moe_out = jnp.dot(weighted, expert_out.astype(f32), precision=lax.Precision.HIGHEST)
    mixed = jnp.where(live_rows[:, None], hidden_state.astype(f32) + moe_out, 0.0)
    return mixed.astype(bf16)


def solution(mesh):
    in_specs = (
        P(("grp", "ep"), None),
        P(("grp", "ep"), None),
        P(("grp", "ep"), None),
        P(),
        P(),
        P("grp", "ep", None, None, None),
        P("grp", "ep"),
        P("grp", "ep"),
        P(None, "grp"),
        P(("grp", "ep"), None),
        P(),
        P(("grp", "ep"), None),
        P(("grp", "ep"), None),
        P(None, None, ("grp", "ep")),
        P(("grp", "ep"), None),
    )
    out_specs = P(("grp", "ep"), None)
    return jax.shard_map(
        per_device, mesh=mesh, in_specs=in_specs, out_specs=out_specs, check_vma=False
    )
```

```python
import functools
import math

import jax
import jax.numpy as jnp
from jax import lax
from jax.experimental import pallas as pl
from jax.experimental.pallas import tpu as pltpu
from jax.sharding import PartitionSpec as P

theta_base = 1000000.0
eps_norm = 1e-06
f32 = jnp.float32
bf16 = jnp.bfloat16


def normed(values, scales):
    return values * lax.rsqrt(jnp.mean(values * values, axis=-1, keepdims=True) + eps_norm) * scales


def rotation_tables(position, head_width):
    half_width = head_width // 2
    inv_freq = jnp.power(theta_base, -2.0 * jnp.arange(half_width, dtype=f32) / head_width)
    angles = position[:, None] * inv_freq[None, :]
    cosine, sine = jnp.cos(angles), jnp.sin(angles)
    return jnp.concatenate([cosine, cosine], -1), jnp.concatenate([-sine, sine], -1)


def attention_body(
    kv_heads, cache_rows, len_ref, own_ref, q_ref, k_ref, v_ref, qg_ref, kg_ref, cos_ref, sin_ref, kv_ref, tag_ref, out_ref
):
    tok_count = q_ref.shape[0]
    hd = qg_ref.shape[1]
    width = kv_heads * hd
    group = q_ref.shape[1] // width
    rows = group * tok_count
    scaling = 1.0 / math.sqrt(hd)
    seq_len = len_ref[0, 0]
    start = pl.multiple_of(own_ref[0, 0] * cache_rows, cache_rows)
    cosine, sine = cos_ref[...], sin_ref[...]

    def prepared(raw, gain):
        values = normed(raw.astype(f32), gain)
        return (values * cosine + pltpu.roll(values, hd // 2, 1) * sine).astype(bf16)

    slot = lax.broadcasted_iota(jnp.int32, (rows, tok_count), 0) % tok_count
    other = lax.broadcasted_iota(jnp.int32, (rows, tok_count), 1)
    causal = (other <= slot) & (other < seq_len)
    live = lax.broadcasted_iota(jnp.int32, (rows, hd), 0) % tok_count < seq_len
    contract = (((1,), (1,)), ((), ()))

    def weighed(queries, keys):
        return jnp.exp(lax.dot_general(queries, keys, contract, preferred_element_type=f32) * scaling)

    out_ref[:, pl.ds(q_ref.shape[1], tag_ref.shape[1])] = tag_ref[...]
    for h in range(kv_heads):
        span = pl.ds(h * hd, hd)
        queries = jnp.concatenate(
            [prepared(q_ref[:, pl.ds((h * group + j) * hd, hd)], qg_ref[...]) for j in range(group)], 0
        )
        pre = weighed(queries, kv_ref[:, span])
        cont = weighed(queries, kv_ref[pl.ds(start, cache_rows), pl.ds(2 * width + h * hd, hd)])
        own = jnp.where(causal, weighed(queries, prepared(k_ref[:, span], kg_ref[...])), 0.0)
        numerator = (
            jnp.dot(pre.astype(bf16), kv_ref[:, pl.ds(width + h * hd, hd)], preferred_element_type=f32)
            + jnp.dot(
                cont.astype(bf16),
                kv_ref[pl.ds(start, cache_rows), pl.ds(3 * width + h * hd, hd)],
                preferred_element_type=f32,
            )
            + jnp.dot(own.astype(bf16), v_ref[:, span], preferred_element_type=f32)
        )
        denominator = (
            jnp.sum(pre, 1, keepdims=True) + jnp.sum(cont, 1, keepdims=True) + jnp.sum(own, 1, keepdims=True)
        )
        result = jnp.where(live, numerator / denominator, 0.0).astype(bf16)
        for j in range(group):
            out_ref[:, pl.ds((h * group + j) * hd, hd)] = result[j * tok_count : (j + 1) * tok_count]


def attention(q_raw, k_raw, v_raw, q_gain, k_gain, kv_block, tag, lengths, cont_owner, cache_rows):
    hd = q_gain.shape[0]
    tok_count = q_raw.shape[0]
    position = (kv_block.shape[0] + cache_rows + jnp.arange(tok_count, dtype=jnp.int32)).astype(f32)
    cosine, sine = rotation_tables(position, hd)
    vmem = pl.BlockSpec(memory_space=pltpu.VMEM)
    smem = pl.BlockSpec(memory_space=pltpu.SMEM)
    return pl.pallas_call(
        functools.partial(attention_body, k_raw.shape[1] // hd, cache_rows),
        out_shape=jax.ShapeDtypeStruct((tok_count, q_raw.shape[1] + tag.shape[1]), bf16),
        in_specs=[smem, smem] + [vmem] * 9,
        out_specs=vmem,
    )(lengths, cont_owner, q_raw, k_raw, v_raw, q_gain[None], k_gain[None], cosine, sine, kv_block, tag)


def per_device(
    q_raw,
    k_raw,
    v_raw,
    q_gain,
    k_gain,
    caches,
    lengths,
    cont_owner,
    out_weight,
    residual,
    moe_gain,
    routes,
    gate_weights,
    w_in,
    w_down,
):
    n_groups = lax.axis_size("grp")
    n_columns = lax.axis_size("ep")
    tok_count, model_width = residual.shape
    heads_width = q_raw.shape[1]
    cache_rows = caches.shape[1]
    top_count = routes.shape[1]
    pieces = 4
    cores = 2
    half = model_width // cores
    expert_count = n_groups * n_columns // pieces
    local = expert_count // n_groups
    capacity = 2
    group_slots = local * capacity
    per_source = n_groups * capacity
    core = lax.axis_index("grp") % cores
    live_rows = jnp.arange(tok_count, dtype=jnp.int32) < lengths[0, 0]

    trades = []
    for g in range(n_groups):
        for p in range(n_columns):
            to = (g - g % 2 + p % 2) * n_columns + p - p % 2 + g % 2
            trades.append((g * n_columns + p, to))
    w_in = lax.ppermute(w_in, ("grp", "ep"), trades)
    w_down = lax.ppermute(w_down, ("grp", "ep"), trades)
    swap = [(g, g ^ 1) for g in range(n_groups)]

    flat_route = jnp.where(live_rows[:, None], routes, -1).reshape(-1)
    assign_idx = jnp.arange(flat_route.shape[0], dtype=jnp.int32)
    matches = (flat_route[:, None] == flat_route[None, :]) & (assign_idx[None, :] < assign_idx[:, None])
    slot_rank = jnp.sum(matches.astype(jnp.int32), axis=1)
    place = jnp.where(flat_route >= 0, flat_route * capacity + slot_rank, -1)
    slots = jnp.arange(expert_count * capacity, dtype=jnp.int32)
    placed = place.reshape(tok_count, top_count, 1) == slots
    weighted = jnp.sum(jnp.where(placed, gate_weights[:, :, None], 0.0), axis=1)
    chosen = jnp.any(placed, axis=1)
    holder = jnp.sum(
        jnp.where(chosen, jnp.arange(1, tok_count + 1, dtype=jnp.int32)[:, None], 0), axis=0
    ) - 1
    tag = jnp.pad(holder.reshape(n_groups, group_slots).astype(bf16), ((0, 0), (0, 128 - group_slots)))

    kv_block = lax.all_gather(caches.reshape(cache_rows, -1), "ep", axis=0, tiled=True)
    kv_block, w_in, w_down = lax.optimization_barrier((kv_block, w_in, w_down))
    own_at, other_at = core * half, (1 - core) * half
    w_in_own = lax.dynamic_slice_in_dim(w_in, own_at, half, 1)
    w_in_other = lax.dynamic_slice_in_dim(w_in, other_at, half, 1)
    w_down_own = lax.dynamic_slice_in_dim(w_down, own_at, half, 1)
    w_down_other = lax.dynamic_slice_in_dim(w_down, other_at, half, 1)
    attended = attention(q_raw, k_raw, v_raw, q_gain, k_gain, kv_block, tag, lengths, cont_owner, cache_rows)
    gathered = lax.all_gather(attended, "grp", axis=0, tiled=True)
    projected = jnp.dot(gathered[:, :heads_width], out_weight, preferred_element_type=f32).astype(bf16)
    attn_proj = lax.all_to_all(projected, "grp", split_axis=0, concat_axis=1, tiled=True)
    hidden_state = (residual.astype(f32) + attn_proj.astype(f32)).astype(bf16)
    moe_in = normed(hidden_state.astype(f32), moe_gain).astype(bf16)

    holders = gathered[:, heads_width : heads_width + group_slots].astype(jnp.int32)
    holders = holders.reshape(n_groups, n_groups, group_slots)
    mine = lax.dynamic_slice_in_dim(holders, lax.axis_index("grp") - core, cores, 1)
    mine = mine.reshape(n_groups, cores, local, capacity).transpose(2, 1, 0, 3)
    source_row = (jnp.arange(n_groups, dtype=jnp.int32) * tok_count)[:, None]
    wanted = jnp.where(mine >= 0, mine + source_row, -1)
    wanted = jnp.broadcast_to(wanted[:, None], (local, pieces // cores) + wanted.shape[1:]).reshape(-1)
    select = (wanted[:, None] == jnp.arange(n_groups * tok_count, dtype=jnp.int32)[None, :]).astype(bf16)

    tokens = lax.all_gather(moe_in, "grp", axis=0, tiled=True)
    outgoing = jnp.dot(
        select, lax.dynamic_slice_in_dim(tokens, own_at, half, 1), preferred_element_type=f32
    ).astype(bf16)
    received = lax.all_to_all(
        outgoing.reshape(n_columns, per_source, half), "ep", split_axis=0, concat_axis=0, tiled=True
    ).reshape(-1, half)
    partner = lax.ppermute(received, "grp", swap)

    def project(which):
        return jnp.dot(received, w_in_own[which], preferred_element_type=f32) + jnp.dot(
            partner, w_in_other[which], preferred_element_type=f32
        )

    inner_act = (jax.nn.silu(project(0)) * project(1)).astype(bf16)
    for_partner = jnp.dot(inner_act, w_down_other, preferred_element_type=f32).astype(bf16)
    from_partner = lax.ppermute(for_partner, "grp", swap)
    partial_out = jnp.dot(inner_act, w_down_own, preferred_element_type=f32)
    partial_out = (partial_out + from_partner.astype(f32)).astype(bf16)
    returned = lax.all_to_all(
        partial_out.reshape(n_columns, per_source, half), "ep", split_axis=0, concat_axis=0, tiled=True
    ).reshape(-1, half)
    in_row = jnp.arange(n_columns * per_source, dtype=jnp.int32)
    in_slot, in_column = in_row % per_source, in_row // per_source
    target = (
        in_slot // capacity * (cores * group_slots)
        + in_column % cores * group_slots
        + in_column // pieces * capacity
        + in_slot % capacity
    )
    out_row = jnp.arange(n_groups * cores * group_slots, dtype=jnp.int32)
    gather_sum = (out_row[:, None] == target[None, :]).astype(bf16)
    summed = jnp.dot(gather_sum, returned, preferred_element_type=f32).astype(bf16)
    expert_out = lax.all_to_all(
        summed.reshape(n_groups, cores * group_slots, half), "grp", split_axis=0, concat_axis=0, tiled=True
    )
    expert_out = expert_out.reshape(n_groups // cores, cores, cores * group_slots, half).astype(f32)
    moe_out = jnp.concatenate(
        [
            jnp.dot(weighted, expert_out[:, c].reshape(-1, half), precision=lax.Precision.HIGHEST)
            for c in range(cores)
        ],
        axis=1,
    )
    mixed = jnp.where(live_rows[:, None], hidden_state.astype(f32) + moe_out, 0.0)
    return mixed.astype(bf16)


def solution(mesh):
    in_specs = (
        P(("grp", "ep"), None),
        P(("grp", "ep"), None),
        P(("grp", "ep"), None),
        P(),
        P(),
        P("grp", "ep", None, None, None),
        P("grp", "ep"),
        P("grp", "ep"),
        P(None, "grp"),
        P(("grp", "ep"), None),
        P(),
        P(("grp", "ep"), None),
        P(("grp", "ep"), None),
        P(None, None, ("grp", "ep")),
        P(("grp", "ep"), None),
    )
    out_specs = P(("grp", "ep"), None)
    return jax.shard_map(
        per_device, mesh=mesh, in_specs=in_specs, out_specs=out_specs, check_vma=False
    )
```

```python
import functools
import math

import jax
import jax.numpy as jnp
from jax import lax
from jax.experimental import pallas as pl
from jax.experimental.pallas import tpu as pltpu
from jax.sharding import PartitionSpec as P

theta_base = 1000000.0
eps_norm = 1e-06
f32 = jnp.float32
bf16 = jnp.bfloat16


def normed(values, scales):
    return values * lax.rsqrt(jnp.mean(values * values, axis=-1, keepdims=True) + eps_norm) * scales


def rotation_tables(position, head_width):
    half_width = head_width // 2
    inv_freq = jnp.power(theta_base, -2.0 * jnp.arange(half_width, dtype=f32) / head_width)
    angles = position[:, None] * inv_freq[None, :]
    cosine, sine = jnp.cos(angles), jnp.sin(angles)
    return jnp.concatenate([cosine, cosine], -1), jnp.concatenate([-sine, sine], -1)


MESH = pl.DeviceIdType.MESH


class Flights:
    def __init__(self, send_sems, recv_sems):
        self.sems = send_sems, recv_sems
        self.copies = []

    def send(self, src, dst, device):
        at = len(self.copies)
        copy = pltpu.make_async_remote_copy(
            src, dst, self.sems[0].at[at], self.sems[1].at[at], device_id=device, device_id_type=MESH
        )
        copy.start()
        self.copies.append(copy)
        return copy

    def finish(self):
        for copy in self.copies:
            copy.wait_send()


def greet(devices):
    barrier = pltpu.get_barrier_semaphore()
    for device in devices:
        pl.semaphore_signal(barrier, inc=1, device_id=device, device_id_type=MESH)
    pl.semaphore_wait(barrier, len(devices))


def ring_order(n):
    order = [0]
    for step in range(1, n // 2 + 1):
        order.append(-step)
        if step < n - n // 2:
            order.append(step)
    return order


def column_gather_body(columns, in_ref, out_ref, local_sem, send_sems, recv_sems):
    g, p = lax.axis_index("grp"), lax.axis_index("ep")
    n_x = lax.axis_size("ep") // columns
    x, y = p // columns, p % columns
    half = in_ref.shape[0] // 2
    up = (g, x * columns + (y + 1) % columns)
    down = (g, x * columns + (y + columns - 1) % columns)
    right = (g, (x + 1) % n_x * columns + y)
    left = (g, (x + n_x - 1) % n_x * columns + y)
    greet([up, down, right, left])
    flights = Flights(send_sems, recv_sems)
    local = pltpu.make_async_copy(in_ref, out_ref.at[p], local_sem)
    local.start()

    def block(across, along):
        return (x + across + n_x) % n_x * columns + (y + along + columns) % columns

    coming, sideways = {}, []
    order = ring_order(columns)
    for along in order:
        here = out_ref.at[block(0, along)]
        if along == 0:
            source = in_ref
        else:
            coming[along].wait_recv()
            source = here
        if along <= 0 and along - 1 in order:
            coming[along - 1] = flights.send(source, here, up)
        if along >= 0 and along + 1 in order:
            coming[along + 1] = flights.send(source, here, down)
        sideways.append((flights.send(source, here, right), flights.send(source, here, left)))
    last = []
    for along, (from_left, from_right) in zip(order, sideways):
        from_left.wait_recv()
        part = out_ref.at[block(-1, along), pl.ds(0, half)]
        last.append(flights.send(part, part, right))
        from_right.wait_recv()
        part = out_ref.at[block(1, along), pl.ds(half, half)]
        last.append(flights.send(part, part, left))
    for copy in last:
        copy.wait_recv()
    local.wait()
    flights.finish()


def column_gather(rows, columns, n_columns):
    count = columns - 1 + 4 * columns
    vmem = pl.BlockSpec(memory_space=pltpu.VMEM)
    gathered = pl.pallas_call(
        functools.partial(column_gather_body, columns),
        out_shape=jax.ShapeDtypeStruct((n_columns,) + rows.shape, rows.dtype),
        in_specs=[vmem],
        out_specs=vmem,
        scratch_shapes=[
            pltpu.SemaphoreType.DMA,
            pltpu.SemaphoreType.DMA((count,)),
            pltpu.SemaphoreType.DMA((count,)),
        ],
        compiler_params=pltpu.CompilerParams(collective_id=0, has_side_effects=True),
        cost_estimate=pl.CostEstimate(flops=10**9, bytes_accessed=1 << 27, transcendentals=0),
    )(rows)
    return gathered.reshape(-1, rows.shape[1])


def group_places():
    g, p = lax.axis_index("grp"), lax.axis_index("ep")
    depth = lax.axis_size("grp") // 2
    z, core = g // 2, g % 2
    up = ((z + 1) % depth * 2 + core, p)
    down = ((z + depth - 1) % depth * 2 + core, p)
    partner = (z * 2 + 1 - core, p)
    return g, depth, z, core, up, down, partner


def group_gather_body(in_ref, out_ref, local_sem, send_sems, recv_sems):
    g, depth, z, core, up, down, partner = group_places()
    greet([up, down, partner])
    flights = Flights(send_sems, recv_sems)
    local = pltpu.make_async_copy(in_ref, out_ref.at[g], local_sem)
    local.start()
    coming, handed = {}, []
    order = ring_order(depth)
    for along in order:
        here = out_ref.at[(z + along + depth) % depth * 2 + core]
        if along == 0:
            source = in_ref
        else:
            coming[along].wait_recv()
            source = here
        if along <= 0 and along - 1 in order:
            coming[along - 1] = flights.send(source, here, up)
        if along >= 0 and along + 1 in order:
            coming[along + 1] = flights.send(source, here, down)
        handed.append(flights.send(source, here, partner))
    for copy in handed:
        copy.wait_recv()
    local.wait()
    flights.finish()


def half_gather_body(in_ref, out_ref, local_sem, send_sems, recv_sems):
    g, depth, z, core, up, down, partner = group_places()
    half = out_ref.shape[2]
    greet([up, down, partner])
    flights = Flights(send_sems, recv_sems)
    own = in_ref.at[:, pl.ds(pl.multiple_of(core * half, half), half)]
    other = in_ref.at[:, pl.ds(pl.multiple_of((1 - core) * half, half), half)]
    swapped = flights.send(other, out_ref.at[g], partner)
    local = pltpu.make_async_copy(own, out_ref.at[g], local_sem)
    local.start()
    swapped.wait_recv()
    local.wait()
    coming = {}
    order = ring_order(depth)
    for along in order:
        here = out_ref.at[pl.ds((z + along + depth) % depth * 2, 2)]
        if along != 0:
            coming[along].wait_recv()
        if along <= 0 and along - 1 in order:
            coming[along - 1] = flights.send(here, here, up)
        if along >= 0 and along + 1 in order:
            coming[along + 1] = flights.send(here, here, down)
    flights.finish()


def over_groups(body, count, width, collective_id, rows):
    n_groups = lax.axis_size("grp")
    vmem = pl.BlockSpec(memory_space=pltpu.VMEM)
    gathered = pl.pallas_call(
        body,
        out_shape=jax.ShapeDtypeStruct((n_groups, rows.shape[0], width), rows.dtype),
        in_specs=[vmem],
        out_specs=vmem,
        scratch_shapes=[
            pltpu.SemaphoreType.DMA,
            pltpu.SemaphoreType.DMA((count,)),
            pltpu.SemaphoreType.DMA((count,)),
        ],
        compiler_params=pltpu.CompilerParams(collective_id=collective_id, has_side_effects=True),
    )(rows)
    return gathered.reshape(-1, width)


def group_gather(rows):
    return over_groups(group_gather_body, lax.axis_size("grp") - 1, rows.shape[1], 1, rows)


def half_gather(rows):
    return over_groups(half_gather_body, lax.axis_size("grp") // 2, rows.shape[1] // 2, 2, rows)


def attention_body(
    kv_heads, cache_rows, len_ref, own_ref, q_ref, k_ref, v_ref, qg_ref, kg_ref, cos_ref, sin_ref, kv_ref, tag_ref, out_ref
):
    tok_count = q_ref.shape[0]
    hd = qg_ref.shape[1]
    width = kv_heads * hd
    group = q_ref.shape[1] // width
    rows = group * tok_count
    scaling = 1.0 / math.sqrt(hd)
    seq_len = len_ref[0, 0]
    start = pl.multiple_of(own_ref[0, 0] * cache_rows, cache_rows)
    cosine, sine = cos_ref[...], sin_ref[...]

    def prepared(raw, gain):
        values = normed(raw.astype(f32), gain)
        return (values * cosine + pltpu.roll(values, hd // 2, 1) * sine).astype(bf16)

    slot = lax.broadcasted_iota(jnp.int32, (rows, tok_count), 0) % tok_count
    other = lax.broadcasted_iota(jnp.int32, (rows, tok_count), 1)
    causal = (other <= slot) & (other < seq_len)
    live = lax.broadcasted_iota(jnp.int32, (rows, hd), 0) % tok_count < seq_len
    contract = (((1,), (1,)), ((), ()))

    def weighed(queries, keys):
        return jnp.exp(lax.dot_general(queries, keys, contract, preferred_element_type=f32) * scaling)

    out_ref[:, pl.ds(q_ref.shape[1], tag_ref.shape[1])] = tag_ref[...]
    for h in range(kv_heads):
        span = pl.ds(h * hd, hd)
        queries = jnp.concatenate(
            [prepared(q_ref[:, pl.ds((h * group + j) * hd, hd)], qg_ref[...]) for j in range(group)], 0
        )
        pre = weighed(queries, kv_ref[:, span])
        cont = weighed(queries, kv_ref[pl.ds(start, cache_rows), pl.ds(2 * width + h * hd, hd)])
        own = jnp.where(causal, weighed(queries, prepared(k_ref[:, span], kg_ref[...])), 0.0)
        numerator = (
            jnp.dot(pre.astype(bf16), kv_ref[:, pl.ds(width + h * hd, hd)], preferred_element_type=f32)
            + jnp.dot(
                cont.astype(bf16),
                kv_ref[pl.ds(start, cache_rows), pl.ds(3 * width + h * hd, hd)],
                preferred_element_type=f32,
            )
            + jnp.dot(own.astype(bf16), v_ref[:, span], preferred_element_type=f32)
        )
        denominator = (
            jnp.sum(pre, 1, keepdims=True) + jnp.sum(cont, 1, keepdims=True) + jnp.sum(own, 1, keepdims=True)
        )
        result = jnp.where(live, numerator / denominator, 0.0).astype(bf16)
        for j in range(group):
            out_ref[:, pl.ds((h * group + j) * hd, hd)] = result[j * tok_count : (j + 1) * tok_count]


def attention(q_raw, k_raw, v_raw, q_gain, k_gain, kv_block, tag, lengths, cont_owner, cache_rows):
    hd = q_gain.shape[0]
    tok_count = q_raw.shape[0]
    position = (kv_block.shape[0] + cache_rows + jnp.arange(tok_count, dtype=jnp.int32)).astype(f32)
    cosine, sine = rotation_tables(position, hd)
    vmem = pl.BlockSpec(memory_space=pltpu.VMEM)
    smem = pl.BlockSpec(memory_space=pltpu.SMEM)
    return pl.pallas_call(
        functools.partial(attention_body, k_raw.shape[1] // hd, cache_rows),
        out_shape=jax.ShapeDtypeStruct((tok_count, q_raw.shape[1] + tag.shape[1]), bf16),
        in_specs=[smem, smem] + [vmem] * 9,
        out_specs=vmem,
    )(lengths, cont_owner, q_raw, k_raw, v_raw, q_gain[None], k_gain[None], cosine, sine, kv_block, tag)


def per_device(
    q_raw,
    k_raw,
    v_raw,
    q_gain,
    k_gain,
    caches,
    lengths,
    cont_owner,
    out_weight,
    residual,
    moe_gain,
    routes,
    gate_weights,
    w_in,
    w_down,
):
    n_groups = lax.axis_size("grp")
    n_columns = lax.axis_size("ep")
    tok_count, model_width = residual.shape
    heads_width = q_raw.shape[1]
    cache_rows = caches.shape[1]
    top_count = routes.shape[1]
    pieces = 4
    cores = 2
    ring_columns = 8
    half = model_width // cores
    expert_count = n_groups * n_columns // pieces
    local = expert_count // n_groups
    capacity = 2
    group_slots = local * capacity
    per_source = n_groups * capacity
    core = lax.axis_index("grp") % cores
    live_rows = jnp.arange(tok_count, dtype=jnp.int32) < lengths[0, 0]

    trades = []
    for g in range(n_groups):
        for p in range(n_columns):
            to = (g - g % 2 + p % 2) * n_columns + p - p % 2 + g % 2
            trades.append((g * n_columns + p, to))
    w_in = lax.ppermute(w_in, ("grp", "ep"), trades)
    w_down = lax.ppermute(w_down, ("grp", "ep"), trades)
    swap = [(g, g ^ 1) for g in range(n_groups)]

    flat_route = jnp.where(live_rows[:, None], routes, -1).reshape(-1)
    assign_idx = jnp.arange(flat_route.shape[0], dtype=jnp.int32)
    matches = (flat_route[:, None] == flat_route[None, :]) & (assign_idx[None, :] < assign_idx[:, None])
    slot_rank = jnp.sum(matches.astype(jnp.int32), axis=1)
    place = jnp.where(flat_route >= 0, flat_route * capacity + slot_rank, -1)
    slots = jnp.arange(expert_count * capacity, dtype=jnp.int32)
    placed = place.reshape(tok_count, top_count, 1) == slots
    weighted = jnp.sum(jnp.where(placed, gate_weights[:, :, None], 0.0), axis=1)
    chosen = jnp.any(placed, axis=1)
    holder = jnp.sum(
        jnp.where(chosen, jnp.arange(1, tok_count + 1, dtype=jnp.int32)[:, None], 0), axis=0
    ) - 1
    tag = jnp.pad(holder.reshape(n_groups, group_slots).astype(bf16), ((0, 0), (0, 128 - group_slots)))

    kv_block = column_gather(caches.reshape(cache_rows, -1), ring_columns, n_columns)
    kv_block, w_in, w_down = lax.optimization_barrier((kv_block, w_in, w_down))
    own_at, other_at = core * half, (1 - core) * half
    w_in_own = lax.dynamic_slice_in_dim(w_in, own_at, half, 1)
    w_in_other = lax.dynamic_slice_in_dim(w_in, other_at, half, 1)
    w_down_own = lax.dynamic_slice_in_dim(w_down, own_at, half, 1)
    w_down_other = lax.dynamic_slice_in_dim(w_down, other_at, half, 1)
    attended = attention(q_raw, k_raw, v_raw, q_gain, k_gain, kv_block, tag, lengths, cont_owner, cache_rows)
    gathered = group_gather(attended)
    projected = jnp.dot(gathered[:, :heads_width], out_weight, preferred_element_type=f32).astype(bf16)
    attn_proj = lax.all_to_all(projected, "grp", split_axis=0, concat_axis=1, tiled=True)
    hidden_state = (residual.astype(f32) + attn_proj.astype(f32)).astype(bf16)
    moe_in = normed(hidden_state.astype(f32), moe_gain).astype(bf16)

    holders = gathered[:, heads_width : heads_width + group_slots].astype(jnp.int32)
    holders = holders.reshape(n_groups, n_groups, group_slots)
    mine = lax.dynamic_slice_in_dim(holders, lax.axis_index("grp") - core, cores, 1)
    mine = mine.reshape(n_groups, cores, local, capacity).transpose(2, 1, 0, 3)
    source_row = (jnp.arange(n_groups, dtype=jnp.int32) * tok_count)[:, None]
    wanted = jnp.where(mine >= 0, mine + source_row, -1)
    wanted = jnp.broadcast_to(wanted[:, None], (local, pieces // cores) + wanted.shape[1:]).reshape(-1)
    select = (wanted[:, None] == jnp.arange(n_groups * tok_count, dtype=jnp.int32)[None, :]).astype(bf16)

    outgoing = jnp.dot(select, half_gather(moe_in), preferred_element_type=f32).astype(bf16)
    received = lax.all_to_all(
        outgoing.reshape(n_columns, per_source, half), "ep", split_axis=0, concat_axis=0, tiled=True
    ).reshape(-1, half)
    partner = lax.ppermute(received, "grp", swap)

    def project(which):
        return jnp.dot(received, w_in_own[which], preferred_element_type=f32) + jnp.dot(
            partner, w_in_other[which], preferred_element_type=f32
        )

    inner_act = (jax.nn.silu(project(0)) * project(1)).astype(bf16)
    for_partner = jnp.dot(inner_act, w_down_other, preferred_element_type=f32).astype(bf16)
    from_partner = lax.ppermute(for_partner, "grp", swap)
    partial_out = jnp.dot(inner_act, w_down_own, preferred_element_type=f32)
    partial_out = (partial_out + from_partner.astype(f32)).astype(bf16)
    returned = lax.all_to_all(
        partial_out.reshape(n_columns, per_source, half), "ep", split_axis=0, concat_axis=0, tiled=True
    ).reshape(-1, half)
    in_row = jnp.arange(n_columns * per_source, dtype=jnp.int32)
    in_slot, in_column = in_row % per_source, in_row // per_source
    target = (
        in_slot // capacity * (cores * group_slots)
        + in_column % cores * group_slots
        + in_column // pieces * capacity
        + in_slot % capacity
    )
    out_row = jnp.arange(n_groups * cores * group_slots, dtype=jnp.int32)
    gather_sum = (out_row[:, None] == target[None, :]).astype(bf16)
    summed = jnp.dot(gather_sum, returned, preferred_element_type=f32).astype(bf16)
    expert_out = lax.all_to_all(
        summed.reshape(n_groups, cores * group_slots, half), "grp", split_axis=0, concat_axis=0, tiled=True
    )
    expert_out = expert_out.reshape(n_groups // cores, cores, cores * group_slots, half).astype(f32)
    moe_out = jnp.concatenate(
        [
            jnp.dot(weighted, expert_out[:, c].reshape(-1, half), precision=lax.Precision.HIGHEST)
            for c in range(cores)
        ],
        axis=1,
    )
    mixed = jnp.where(live_rows[:, None], hidden_state.astype(f32) + moe_out, 0.0)
    return mixed.astype(bf16)


def solution(mesh):
    in_specs = (
        P(("grp", "ep"), None),
        P(("grp", "ep"), None),
        P(("grp", "ep"), None),
        P(),
        P(),
        P("grp", "ep", None, None, None),
        P("grp", "ep"),
        P("grp", "ep"),
        P(None, "grp"),
        P(("grp", "ep"), None),
        P(),
        P(("grp", "ep"), None),
        P(("grp", "ep"), None),
        P(None, None, ("grp", "ep")),
        P(("grp", "ep"), None),
    )
    out_specs = P(("grp", "ep"), None)
    return jax.shard_map(
        per_device, mesh=mesh, in_specs=in_specs, out_specs=out_specs, check_vma=False
    )
```

```python
import functools
import math

import jax
import jax.numpy as jnp
from jax import lax
from jax.experimental import pallas as pl
from jax.experimental.pallas import tpu as pltpu
from jax.sharding import PartitionSpec as P

theta_base = 1000000.0
eps_norm = 1e-06
f32 = jnp.float32
bf16 = jnp.bfloat16


def normed(values, scales):
    return values * lax.rsqrt(jnp.mean(values * values, axis=-1, keepdims=True) + eps_norm) * scales


def rotation_tables(position, head_width):
    half_width = head_width // 2
    inv_freq = jnp.power(theta_base, -2.0 * jnp.arange(half_width, dtype=f32) / head_width)
    angles = position[:, None] * inv_freq[None, :]
    cosine, sine = jnp.cos(angles), jnp.sin(angles)
    return jnp.concatenate([cosine, cosine], -1), jnp.concatenate([-sine, sine], -1)


MESH = pl.DeviceIdType.MESH


class Flights:
    def __init__(self, send_sems, recv_sems):
        self.sems = send_sems, recv_sems
        self.copies = []

    def send(self, src, dst, device):
        at = len(self.copies)
        copy = pltpu.make_async_remote_copy(
            src, dst, self.sems[0].at[at], self.sems[1].at[at], device_id=device, device_id_type=MESH
        )
        copy.start()
        self.copies.append(copy)
        return copy

    def finish(self):
        for copy in self.copies:
            copy.wait_send()


def greet(devices):
    barrier = pltpu.get_barrier_semaphore()
    for device in devices:
        pl.semaphore_signal(barrier, inc=1, device_id=device, device_id_type=MESH)
    pl.semaphore_wait(barrier, len(devices))


def ring_order(n):
    order = [0]
    for step in range(1, n // 2 + 1):
        order.append(-step)
        if step < n - n // 2:
            order.append(step)
    return order


def column_gather_body(columns, in_ref, out_ref, local_sem, send_sems, recv_sems):
    g, p = lax.axis_index("grp"), lax.axis_index("ep")
    n_x = lax.axis_size("ep") // columns
    x, y = p // columns, p % columns
    half = in_ref.shape[0] // 2
    up = (g, x * columns + (y + 1) % columns)
    down = (g, x * columns + (y + columns - 1) % columns)
    right = (g, (x + 1) % n_x * columns + y)
    left = (g, (x + n_x - 1) % n_x * columns + y)
    greet([up, down, right, left])
    flights = Flights(send_sems, recv_sems)
    local = pltpu.make_async_copy(in_ref, out_ref.at[p], local_sem)
    local.start()

    def block(across, along):
        return (x + across + n_x) % n_x * columns + (y + along + columns) % columns

    coming, sideways = {}, []
    order = ring_order(columns)
    for along in order:
        here = out_ref.at[block(0, along)]
        if along == 0:
            source = in_ref
        else:
            coming[along].wait_recv()
            source = here
        if along <= 0 and along - 1 in order:
            coming[along - 1] = flights.send(source, here, up)
        if along >= 0 and along + 1 in order:
            coming[along + 1] = flights.send(source, here, down)
        sideways.append((flights.send(source, here, right), flights.send(source, here, left)))
    last = []
    for along, (from_left, from_right) in zip(order, sideways):
        from_left.wait_recv()
        part = out_ref.at[block(-1, along), pl.ds(0, half)]
        last.append(flights.send(part, part, right))
        from_right.wait_recv()
        part = out_ref.at[block(1, along), pl.ds(half, half)]
        last.append(flights.send(part, part, left))
    for copy in last:
        copy.wait_recv()
    local.wait()
    flights.finish()


def column_gather(rows, columns, n_columns):
    count = columns - 1 + 4 * columns
    vmem = pl.BlockSpec(memory_space=pltpu.VMEM)
    gathered = pl.pallas_call(
        functools.partial(column_gather_body, columns),
        out_shape=jax.ShapeDtypeStruct((n_columns,) + rows.shape, rows.dtype),
        in_specs=[vmem],
        out_specs=vmem,
        scratch_shapes=[
            pltpu.SemaphoreType.DMA,
            pltpu.SemaphoreType.DMA((count,)),
            pltpu.SemaphoreType.DMA((count,)),
        ],
        compiler_params=pltpu.CompilerParams(collective_id=0, has_side_effects=True),
        cost_estimate=pl.CostEstimate(flops=10**9, bytes_accessed=1 << 27, transcendentals=0),
    )(rows)
    return gathered.reshape(-1, rows.shape[1])


def group_places():
    g, p = lax.axis_index("grp"), lax.axis_index("ep")
    depth = lax.axis_size("grp") // 2
    z, core = g // 2, g % 2
    up = ((z + 1) % depth * 2 + core, p)
    down = ((z + depth - 1) % depth * 2 + core, p)
    partner = (z * 2 + 1 - core, p)
    return g, depth, z, core, up, down, partner


def group_gather_body(in_ref, out_ref, local_sem, send_sems, recv_sems):
    g, depth, z, core, up, down, partner = group_places()
    greet([up, down, partner])
    flights = Flights(send_sems, recv_sems)
    local = pltpu.make_async_copy(in_ref, out_ref.at[g], local_sem)
    local.start()
    coming, handed = {}, []
    order = ring_order(depth)
    lanes = 128
    width = in_ref.shape[1]
    middle = width // lanes // 2 * lanes
    chunks = [pl.ds(0, middle), pl.ds(middle, width - middle)]
    for along in order:
        for c, chunk in enumerate(chunks):
            here = out_ref.at[(z + along + depth) % depth * 2 + core, :, chunk]
            if along == 0:
                source = in_ref.at[:, chunk]
            else:
                coming[along, c].wait_recv()
                source = here
            if along <= 0 and along - 1 in order:
                coming[along - 1, c] = flights.send(source, here, up)
            if along >= 0 and along + 1 in order:
                coming[along + 1, c] = flights.send(source, here, down)
            handed.append(flights.send(source, here, partner))
    for copy in handed:
        copy.wait_recv()
    local.wait()
    flights.finish()


def half_gather_body(in_ref, out_ref, local_sem, send_sems, recv_sems):
    g, depth, z, core, up, down, partner = group_places()
    half = out_ref.shape[2]
    greet([up, down, partner])
    flights = Flights(send_sems, recv_sems)
    own = in_ref.at[:, pl.ds(pl.multiple_of(core * half, half), half)]
    other = in_ref.at[:, pl.ds(pl.multiple_of((1 - core) * half, half), half)]
    swapped = flights.send(other, out_ref.at[g], partner)
    local = pltpu.make_async_copy(own, out_ref.at[g], local_sem)
    local.start()
    swapped.wait_recv()
    local.wait()
    coming = {}
    order = ring_order(depth)
    for along in order:
        here = out_ref.at[pl.ds((z + along + depth) % depth * 2, 2)]
        if along != 0:
            coming[along].wait_recv()
        if along <= 0 and along - 1 in order:
            coming[along - 1] = flights.send(here, here, up)
        if along >= 0 and along + 1 in order:
            coming[along + 1] = flights.send(here, here, down)
    flights.finish()


def over_groups(body, count, width, collective_id, rows):
    n_groups = lax.axis_size("grp")
    vmem = pl.BlockSpec(memory_space=pltpu.VMEM)
    gathered = pl.pallas_call(
        body,
        out_shape=jax.ShapeDtypeStruct((n_groups, rows.shape[0], width), rows.dtype),
        in_specs=[vmem],
        out_specs=vmem,
        scratch_shapes=[
            pltpu.SemaphoreType.DMA,
            pltpu.SemaphoreType.DMA((count,)),
            pltpu.SemaphoreType.DMA((count,)),
        ],
        compiler_params=pltpu.CompilerParams(collective_id=collective_id, has_side_effects=True),
    )(rows)
    return gathered.reshape(-1, width)


def group_gather(rows):
    return over_groups(group_gather_body, 2 * (lax.axis_size("grp") - 1), rows.shape[1], 1, rows)


def half_gather(rows):
    return over_groups(half_gather_body, lax.axis_size("grp") // 2, rows.shape[1] // 2, 2, rows)


def exchange_body(axis, inner, in_ref, out_ref, local_sem, send_sems, recv_sems):
    g, p = lax.axis_index("grp"), lax.axis_index("ep")
    me = lax.axis_index(axis)
    outer = lax.axis_size(axis) // inner
    far = lambda n: sorted(range(n), key=lambda d: (-min(d, n - d), d))
    steps = [(a, b) for b in far(inner) for a in far(outer) if (a, b) != (0, 0)]

    def place(a, b):
        return (me // inner + a) % outer * inner + (me % inner + b) % inner

    peers = [place(a, b) for a, b in steps]
    device = (lambda i: (i, p)) if axis == "grp" else (lambda i: (g, i))
    greet([device(i) for i in peers])
    flights = Flights(send_sems, recv_sems)
    copies = [flights.send(in_ref.at[i], out_ref.at[me], device(i)) for i in peers]
    local = pltpu.make_async_copy(in_ref.at[me], out_ref.at[me], local_sem)
    local.start()
    for copy in copies:
        copy.wait_recv()
    local.wait()
    flights.finish()


def exchange(blocks, axis, inner, collective_id):
    count = blocks.shape[0] - 1
    vmem = pl.BlockSpec(memory_space=pltpu.VMEM)
    return pl.pallas_call(
        functools.partial(exchange_body, axis, inner),
        out_shape=jax.ShapeDtypeStruct(blocks.shape, blocks.dtype),
        in_specs=[vmem],
        out_specs=vmem,
        scratch_shapes=[
            pltpu.SemaphoreType.DMA,
            pltpu.SemaphoreType.DMA((count,)),
            pltpu.SemaphoreType.DMA((count,)),
        ],
        compiler_params=pltpu.CompilerParams(collective_id=collective_id, has_side_effects=True),
    )(blocks)


def attention_body(
    kv_heads, cache_rows, len_ref, own_ref, q_ref, k_ref, v_ref, qg_ref, kg_ref, cos_ref, sin_ref, kv_ref, tag_ref, out_ref
):
    tok_count = q_ref.shape[0]
    hd = qg_ref.shape[1]
    width = kv_heads * hd
    group = q_ref.shape[1] // width
    rows = group * tok_count
    scaling = 1.0 / math.sqrt(hd)
    seq_len = len_ref[0, 0]
    start = pl.multiple_of(own_ref[0, 0] * cache_rows, cache_rows)
    cosine, sine = cos_ref[...], sin_ref[...]

    def prepared(raw, gain):
        values = normed(raw.astype(f32), gain)
        return (values * cosine + pltpu.roll(values, hd // 2, 1) * sine).astype(bf16)

    slot = lax.broadcasted_iota(jnp.int32, (rows, tok_count), 0) % tok_count
    other = lax.broadcasted_iota(jnp.int32, (rows, tok_count), 1)
    causal = (other <= slot) & (other < seq_len)
    live = lax.broadcasted_iota(jnp.int32, (rows, hd), 0) % tok_count < seq_len
    contract = (((1,), (1,)), ((), ()))

    def weighed(queries, keys):
        return jnp.exp(lax.dot_general(queries, keys, contract, preferred_element_type=f32) * scaling)

    out_ref[:, pl.ds(q_ref.shape[1], tag_ref.shape[1])] = tag_ref[...]
    for h in range(kv_heads):
        span = pl.ds(h * hd, hd)
        queries = jnp.concatenate(
            [prepared(q_ref[:, pl.ds((h * group + j) * hd, hd)], qg_ref[...]) for j in range(group)], 0
        )
        pre = weighed(queries, kv_ref[:, span])
        cont = weighed(queries, kv_ref[pl.ds(start, cache_rows), pl.ds(2 * width + h * hd, hd)])
        own = jnp.where(causal, weighed(queries, prepared(k_ref[:, span], kg_ref[...])), 0.0)
        numerator = (
            jnp.dot(pre.astype(bf16), kv_ref[:, pl.ds(width + h * hd, hd)], preferred_element_type=f32)
            + jnp.dot(
                cont.astype(bf16),
                kv_ref[pl.ds(start, cache_rows), pl.ds(3 * width + h * hd, hd)],
                preferred_element_type=f32,
            )
            + jnp.dot(own.astype(bf16), v_ref[:, span], preferred_element_type=f32)
        )
        denominator = (
            jnp.sum(pre, 1, keepdims=True) + jnp.sum(cont, 1, keepdims=True) + jnp.sum(own, 1, keepdims=True)
        )
        result = jnp.where(live, numerator / denominator, 0.0).astype(bf16)
        for j in range(group):
            out_ref[:, pl.ds((h * group + j) * hd, hd)] = result[j * tok_count : (j + 1) * tok_count]


def attention(q_raw, k_raw, v_raw, q_gain, k_gain, kv_block, tag, lengths, cont_owner, cache_rows):
    hd = q_gain.shape[0]
    tok_count = q_raw.shape[0]
    position = (kv_block.shape[0] + cache_rows + jnp.arange(tok_count, dtype=jnp.int32)).astype(f32)
    cosine, sine = rotation_tables(position, hd)
    vmem = pl.BlockSpec(memory_space=pltpu.VMEM)
    smem = pl.BlockSpec(memory_space=pltpu.SMEM)
    return pl.pallas_call(
        functools.partial(attention_body, k_raw.shape[1] // hd, cache_rows),
        out_shape=jax.ShapeDtypeStruct((tok_count, q_raw.shape[1] + tag.shape[1]), bf16),
        in_specs=[smem, smem] + [vmem] * 9,
        out_specs=vmem,
    )(lengths, cont_owner, q_raw, k_raw, v_raw, q_gain[None], k_gain[None], cosine, sine, kv_block, tag)


def per_device(
    q_raw,
    k_raw,
    v_raw,
    q_gain,
    k_gain,
    caches,
    lengths,
    cont_owner,
    out_weight,
    residual,
    moe_gain,
    routes,
    gate_weights,
    w_in,
    w_down,
):
    n_groups = lax.axis_size("grp")
    n_columns = lax.axis_size("ep")
    tok_count, model_width = residual.shape
    heads_width = q_raw.shape[1]
    cache_rows = caches.shape[1]
    top_count = routes.shape[1]
    pieces = 4
    cores = 2
    ring_columns = 8
    half = model_width // cores
    expert_count = n_groups * n_columns // pieces
    local = expert_count // n_groups
    capacity = 2
    group_slots = local * capacity
    per_source = n_groups * capacity
    core = lax.axis_index("grp") % cores
    live_rows = jnp.arange(tok_count, dtype=jnp.int32) < lengths[0, 0]

    trades = []
    for g in range(n_groups):
        for p in range(n_columns):
            to = (g - g % 2 + p % 2) * n_columns + p - p % 2 + g % 2
            trades.append((g * n_columns + p, to))
    w_in = lax.ppermute(w_in, ("grp", "ep"), trades)
    w_down = lax.ppermute(w_down, ("grp", "ep"), trades)
    swap = [(g, g ^ 1) for g in range(n_groups)]

    flat_route = jnp.where(live_rows[:, None], routes, -1).reshape(-1)
    assign_idx = jnp.arange(flat_route.shape[0], dtype=jnp.int32)
    matches = (flat_route[:, None] == flat_route[None, :]) & (assign_idx[None, :] < assign_idx[:, None])
    slot_rank = jnp.sum(matches.astype(jnp.int32), axis=1)
    place = jnp.where(flat_route >= 0, flat_route * capacity + slot_rank, -1)
    slots = jnp.arange(expert_count * capacity, dtype=jnp.int32)
    placed = place.reshape(tok_count, top_count, 1) == slots
    weighted = jnp.sum(jnp.where(placed, gate_weights[:, :, None], 0.0), axis=1)
    chosen = jnp.any(placed, axis=1)
    holder = jnp.sum(
        jnp.where(chosen, jnp.arange(1, tok_count + 1, dtype=jnp.int32)[:, None], 0), axis=0
    ) - 1
    tag = jnp.pad(holder.reshape(n_groups, group_slots).astype(bf16), ((0, 0), (0, 128 - group_slots)))

    kv_block = column_gather(caches.reshape(cache_rows, -1), ring_columns, n_columns)
    kv_block, w_in, w_down = lax.optimization_barrier((kv_block, w_in, w_down))
    own_at, other_at = core * half, (1 - core) * half
    w_in_own = lax.dynamic_slice_in_dim(w_in, own_at, half, 1)
    w_in_other = lax.dynamic_slice_in_dim(w_in, other_at, half, 1)
    w_down_own = lax.dynamic_slice_in_dim(w_down, own_at, half, 1)
    w_down_other = lax.dynamic_slice_in_dim(w_down, other_at, half, 1)
    attended = attention(q_raw, k_raw, v_raw, q_gain, k_gain, kv_block, tag, lengths, cont_owner, cache_rows)
    gathered = group_gather(attended)
    projected = jnp.dot(gathered[:, :heads_width], out_weight, preferred_element_type=f32).astype(bf16)
    attn_proj = exchange(projected.reshape(n_groups, tok_count, -1), "grp", cores, 3)
    attn_proj = attn_proj.transpose(1, 0, 2).reshape(tok_count, model_width)
    hidden_state = (residual.astype(f32) + attn_proj.astype(f32)).astype(bf16)
    moe_in = normed(hidden_state.astype(f32), moe_gain).astype(bf16)

    holders = gathered[:, heads_width : heads_width + group_slots].astype(jnp.int32)
    holders = holders.reshape(n_groups, n_groups, group_slots)
    mine = lax.dynamic_slice_in_dim(holders, lax.axis_index("grp") - core, cores, 1)
    mine = mine.reshape(n_groups, cores, local, capacity).transpose(2, 1, 0, 3)
    source_row = (jnp.arange(n_groups, dtype=jnp.int32) * tok_count)[:, None]
    wanted = jnp.where(mine >= 0, mine + source_row, -1)
    wanted = jnp.broadcast_to(wanted[:, None], (local, pieces // cores) + wanted.shape[1:]).reshape(-1)
    select = (wanted[:, None] == jnp.arange(n_groups * tok_count, dtype=jnp.int32)[None, :]).astype(bf16)

    outgoing = jnp.dot(select, half_gather(moe_in), preferred_element_type=f32).astype(bf16)
    received = exchange(outgoing.reshape(n_columns, per_source, half), "ep", ring_columns, 4).reshape(-1, half)
    partner = lax.ppermute(received, "grp", swap)

    def project(which):
        return jnp.dot(received, w_in_own[which], preferred_element_type=f32) + jnp.dot(
            partner, w_in_other[which], preferred_element_type=f32
        )

    inner_act = (jax.nn.silu(project(0)) * project(1)).astype(bf16)
    for_partner = jnp.dot(inner_act, w_down_other, preferred_element_type=f32).astype(bf16)
    from_partner = lax.ppermute(for_partner, "grp", swap)
    partial_out = jnp.dot(inner_act, w_down_own, preferred_element_type=f32)
    partial_out = (partial_out + from_partner.astype(f32)).astype(bf16)
    returned = exchange(partial_out.reshape(n_columns, per_source, half), "ep", ring_columns, 4).reshape(-1, half)
    in_row = jnp.arange(n_columns * per_source, dtype=jnp.int32)
    in_slot, in_column = in_row % per_source, in_row // per_source
    target = (
        in_slot // capacity * (cores * group_slots)
        + in_column % cores * group_slots
        + in_column // pieces * capacity
        + in_slot % capacity
    )
    out_row = jnp.arange(n_groups * cores * group_slots, dtype=jnp.int32)
    gather_sum = (out_row[:, None] == target[None, :]).astype(bf16)
    summed = jnp.dot(gather_sum, returned, preferred_element_type=f32).astype(bf16)
    expert_out = exchange(summed.reshape(n_groups, cores * group_slots, half), "grp", cores, 5)
    expert_out = expert_out.reshape(n_groups // cores, cores, cores * group_slots, half).astype(f32)
    moe_out = jnp.concatenate(
        [
            jnp.dot(weighted, expert_out[:, c].reshape(-1, half), precision=lax.Precision.HIGHEST)
            for c in range(cores)
        ],
        axis=1,
    )
    mixed = jnp.where(live_rows[:, None], hidden_state.astype(f32) + moe_out, 0.0)
    return mixed.astype(bf16)


def solution(mesh):
    in_specs = (
        P(("grp", "ep"), None),
        P(("grp", "ep"), None),
        P(("grp", "ep"), None),
        P(),
        P(),
        P("grp", "ep", None, None, None),
        P("grp", "ep"),
        P("grp", "ep"),
        P(None, "grp"),
        P(("grp", "ep"), None),
        P(),
        P(("grp", "ep"), None),
        P(("grp", "ep"), None),
        P(None, None, ("grp", "ep")),
        P(("grp", "ep"), None),
    )
    out_specs = P(("grp", "ep"), None)
    return jax.shard_map(
        per_device, mesh=mesh, in_specs=in_specs, out_specs=out_specs, check_vma=False
    )
```

```python
import functools
import math

import jax
import jax.numpy as jnp
from jax import lax
from jax.experimental import pallas as pl
from jax.experimental.pallas import tpu as pltpu
from jax.sharding import PartitionSpec as P

theta_base = 1000000.0
eps_norm = 1e-06
f32 = jnp.float32
bf16 = jnp.bfloat16


def normed(values, scales):
    return values * lax.rsqrt(jnp.mean(values * values, axis=-1, keepdims=True) + eps_norm) * scales


def rotation_tables(position, head_width):
    half_width = head_width // 2
    inv_freq = jnp.power(theta_base, -2.0 * jnp.arange(half_width, dtype=f32) / head_width)
    angles = position[:, None] * inv_freq[None, :]
    cosine, sine = jnp.cos(angles), jnp.sin(angles)
    return jnp.concatenate([cosine, cosine], -1), jnp.concatenate([-sine, sine], -1)


MESH = pl.DeviceIdType.MESH


class Flights:
    def __init__(self, send_sems, recv_sems):
        self.sems = send_sems, recv_sems
        self.copies = []

    def send(self, src, dst, device):
        at = len(self.copies)
        copy = pltpu.make_async_remote_copy(
            src, dst, self.sems[0].at[at], self.sems[1].at[at], device_id=device, device_id_type=MESH
        )
        copy.start()
        self.copies.append(copy)
        return copy

    def finish(self):
        for copy in self.copies:
            copy.wait_send()


def greet(devices):
    barrier = pltpu.get_barrier_semaphore()
    for device in devices:
        pl.semaphore_signal(barrier, inc=1, device_id=device, device_id_type=MESH)
    pl.semaphore_wait(barrier, len(devices))


def ring_order(n):
    order = [0]
    for step in range(1, n // 2 + 1):
        order.append(-step)
        if step < n - n // 2:
            order.append(step)
    return order


def column_gather_body(columns, in_ref, out_ref, local_sem, send_sems, recv_sems):
    g, p = lax.axis_index("grp"), lax.axis_index("ep")
    n_x = lax.axis_size("ep") // columns
    x, y = p // columns, p % columns
    half = in_ref.shape[0] // 2
    up = (g, x * columns + (y + 1) % columns)
    down = (g, x * columns + (y + columns - 1) % columns)
    right = (g, (x + 1) % n_x * columns + y)
    left = (g, (x + n_x - 1) % n_x * columns + y)
    greet([up, down, right, left])
    flights = Flights(send_sems, recv_sems)
    local = pltpu.make_async_copy(in_ref, out_ref.at[p], local_sem)
    local.start()

    def block(across, along):
        return (x + across + n_x) % n_x * columns + (y + along + columns) % columns

    coming, sideways = {}, []
    order = ring_order(columns)
    for along in order:
        here = out_ref.at[block(0, along)]
        if along == 0:
            source = in_ref
        else:
            coming[along].wait_recv()
            source = here
        if along <= 0 and along - 1 in order:
            coming[along - 1] = flights.send(source, here, up)
        if along >= 0 and along + 1 in order:
            coming[along + 1] = flights.send(source, here, down)
        sideways.append((flights.send(source, here, right), flights.send(source, here, left)))
    last = []
    for along, (from_left, from_right) in zip(order, sideways):
        from_left.wait_recv()
        part = out_ref.at[block(-1, along), pl.ds(0, half)]
        last.append(flights.send(part, part, right))
        from_right.wait_recv()
        part = out_ref.at[block(1, along), pl.ds(half, half)]
        last.append(flights.send(part, part, left))
    for copy in last:
        copy.wait_recv()
    local.wait()
    flights.finish()


def column_gather(rows, columns, n_columns):
    count = columns - 1 + 4 * columns
    vmem = pl.BlockSpec(memory_space=pltpu.VMEM)
    gathered = pl.pallas_call(
        functools.partial(column_gather_body, columns),
        out_shape=jax.ShapeDtypeStruct((n_columns,) + rows.shape, rows.dtype),
        in_specs=[vmem],
        out_specs=vmem,
        scratch_shapes=[
            pltpu.SemaphoreType.DMA,
            pltpu.SemaphoreType.DMA((count,)),
            pltpu.SemaphoreType.DMA((count,)),
        ],
        compiler_params=pltpu.CompilerParams(collective_id=0, has_side_effects=True),
        cost_estimate=pl.CostEstimate(flops=10**9, bytes_accessed=1 << 27, transcendentals=0),
    )(rows)
    return gathered.reshape(-1, rows.shape[1])


def group_places():
    g, p = lax.axis_index("grp"), lax.axis_index("ep")
    depth = lax.axis_size("grp") // 2
    z, core = g // 2, g % 2
    up = ((z + 1) % depth * 2 + core, p)
    down = ((z + depth - 1) % depth * 2 + core, p)
    partner = (z * 2 + 1 - core, p)
    return g, depth, z, core, up, down, partner


def group_gather_body(in_ref, out_ref, local_sem, send_sems, recv_sems):
    g, depth, z, core, up, down, partner = group_places()
    greet([up, down, partner])
    flights = Flights(send_sems, recv_sems)
    local = pltpu.make_async_copy(in_ref, out_ref.at[g], local_sem)
    local.start()
    coming, handed = {}, []
    order = ring_order(depth)
    lanes = 128
    width = in_ref.shape[1]
    middle = width // lanes // 2 * lanes
    chunks = [pl.ds(0, middle), pl.ds(middle, width - middle)]
    for along in order:
        for c, chunk in enumerate(chunks):
            here = out_ref.at[(z + along + depth) % depth * 2 + core, :, chunk]
            if along == 0:
                source = in_ref.at[:, chunk]
            else:
                coming[along, c].wait_recv()
                source = here
            if along <= 0 and along - 1 in order:
                coming[along - 1, c] = flights.send(source, here, up)
            if along >= 0 and along + 1 in order:
                coming[along + 1, c] = flights.send(source, here, down)
            handed.append(flights.send(source, here, partner))
    for copy in handed:
        copy.wait_recv()
    local.wait()
    flights.finish()


def half_gather_body(in_ref, out_ref, local_sem, send_sems, recv_sems):
    g, depth, z, core, up, down, partner = group_places()
    half = out_ref.shape[2]
    greet([up, down, partner])
    flights = Flights(send_sems, recv_sems)
    own = in_ref.at[:, pl.ds(pl.multiple_of(core * half, half), half)]
    other = in_ref.at[:, pl.ds(pl.multiple_of((1 - core) * half, half), half)]
    swapped = flights.send(other, out_ref.at[g], partner)
    local = pltpu.make_async_copy(own, out_ref.at[g], local_sem)
    local.start()
    swapped.wait_recv()
    local.wait()
    coming = {}
    order = ring_order(depth)
    for along in order:
        here = out_ref.at[pl.ds((z + along + depth) % depth * 2, 2)]
        if along != 0:
            coming[along].wait_recv()
        if along <= 0 and along - 1 in order:
            coming[along - 1] = flights.send(here, here, up)
        if along >= 0 and along + 1 in order:
            coming[along + 1] = flights.send(here, here, down)
    flights.finish()


def over_groups(body, count, width, collective_id, rows):
    n_groups = lax.axis_size("grp")
    vmem = pl.BlockSpec(memory_space=pltpu.VMEM)
    gathered = pl.pallas_call(
        body,
        out_shape=jax.ShapeDtypeStruct((n_groups, rows.shape[0], width), rows.dtype),
        in_specs=[vmem],
        out_specs=vmem,
        scratch_shapes=[
            pltpu.SemaphoreType.DMA,
            pltpu.SemaphoreType.DMA((count,)),
            pltpu.SemaphoreType.DMA((count,)),
        ],
        compiler_params=pltpu.CompilerParams(collective_id=collective_id, has_side_effects=True),
    )(rows)
    return gathered.reshape(-1, width)


def group_gather(rows):
    return over_groups(group_gather_body, 2 * (lax.axis_size("grp") - 1), rows.shape[1], 1, rows)


def half_gather(rows):
    return over_groups(half_gather_body, lax.axis_size("grp") // 2, rows.shape[1] // 2, 2, rows)


def exchange_body(axis, inner, in_ref, out_ref, local_sem, send_sems, recv_sems):
    g, p = lax.axis_index("grp"), lax.axis_index("ep")
    me = lax.axis_index(axis)
    outer = lax.axis_size(axis) // inner
    far = lambda n: sorted(range(n), key=lambda d: (-min(d, n - d), d))
    steps = [(a, b) for b in far(inner) for a in far(outer) if (a, b) != (0, 0)]

    def place(a, b):
        return (me // inner + a) % outer * inner + (me % inner + b) % inner

    peers = [place(a, b) for a, b in steps]
    device = (lambda i: (i, p)) if axis == "grp" else (lambda i: (g, i))
    greet([device(i) for i in peers])
    flights = Flights(send_sems, recv_sems)
    copies = [flights.send(in_ref.at[i], out_ref.at[me], device(i)) for i in peers]
    local = pltpu.make_async_copy(in_ref.at[me], out_ref.at[me], local_sem)
    local.start()
    for copy in copies:
        copy.wait_recv()
    local.wait()
    flights.finish()


def exchange(blocks, axis, inner, collective_id):
    count = blocks.shape[0] - 1
    vmem = pl.BlockSpec(memory_space=pltpu.VMEM)
    return pl.pallas_call(
        functools.partial(exchange_body, axis, inner),
        out_shape=jax.ShapeDtypeStruct(blocks.shape, blocks.dtype),
        in_specs=[vmem],
        out_specs=vmem,
        scratch_shapes=[
            pltpu.SemaphoreType.DMA,
            pltpu.SemaphoreType.DMA((count,)),
            pltpu.SemaphoreType.DMA((count,)),
        ],
        compiler_params=pltpu.CompilerParams(collective_id=collective_id, has_side_effects=True),
    )(blocks)


def attention_body(
    kv_heads, cache_rows, len_ref, own_ref, q_ref, k_ref, v_ref, qg_ref, kg_ref, cos_ref, sin_ref, kv_ref, tag_ref, out_ref
):
    tok_count = q_ref.shape[0]
    hd = qg_ref.shape[1]
    width = kv_heads * hd
    group = q_ref.shape[1] // width
    rows = group * tok_count
    scaling = 1.0 / math.sqrt(hd)
    seq_len = len_ref[0, 0]
    start = pl.multiple_of(own_ref[0, 0] * cache_rows, cache_rows)
    cosine, sine = cos_ref[...], sin_ref[...]

    def prepared(raw, gain):
        values = normed(raw.astype(f32), gain)
        return (values * cosine + pltpu.roll(values, hd // 2, 1) * sine).astype(bf16)

    slot = lax.broadcasted_iota(jnp.int32, (rows, tok_count), 0) % tok_count
    other = lax.broadcasted_iota(jnp.int32, (rows, tok_count), 1)
    causal = (other <= slot) & (other < seq_len)
    live = lax.broadcasted_iota(jnp.int32, (rows, hd), 0) % tok_count < seq_len
    contract = (((1,), (1,)), ((), ()))

    def weighed(queries, keys):
        return jnp.exp(lax.dot_general(queries, keys, contract, preferred_element_type=f32) * scaling)

    out_ref[:, pl.ds(q_ref.shape[1], tag_ref.shape[1])] = tag_ref[...]
    for h in range(kv_heads):
        span = pl.ds(h * hd, hd)
        queries = jnp.concatenate(
            [prepared(q_ref[:, pl.ds((h * group + j) * hd, hd)], qg_ref[...]) for j in range(group)], 0
        )
        pre = weighed(queries, kv_ref[:, span])
        cont = weighed(queries, kv_ref[pl.ds(start, cache_rows), pl.ds(2 * width + h * hd, hd)])
        own = jnp.where(causal, weighed(queries, prepared(k_ref[:, span], kg_ref[...])), 0.0)
        numerator = (
            jnp.dot(pre.astype(bf16), kv_ref[:, pl.ds(width + h * hd, hd)], preferred_element_type=f32)
            + jnp.dot(
                cont.astype(bf16),
                kv_ref[pl.ds(start, cache_rows), pl.ds(3 * width + h * hd, hd)],
                preferred_element_type=f32,
            )
            + jnp.dot(own.astype(bf16), v_ref[:, span], preferred_element_type=f32)
        )
        denominator = (
            jnp.sum(pre, 1, keepdims=True) + jnp.sum(cont, 1, keepdims=True) + jnp.sum(own, 1, keepdims=True)
        )
        result = jnp.where(live, numerator / denominator, 0.0).astype(bf16)
        for j in range(group):
            out_ref[:, pl.ds((h * group + j) * hd, hd)] = result[j * tok_count : (j + 1) * tok_count]


def attention(q_raw, k_raw, v_raw, q_gain, k_gain, kv_block, tag, lengths, cont_owner, cache_rows):
    hd = q_gain.shape[0]
    tok_count = q_raw.shape[0]
    position = (kv_block.shape[0] + cache_rows + jnp.arange(tok_count, dtype=jnp.int32)).astype(f32)
    cosine, sine = rotation_tables(position, hd)
    vmem = pl.BlockSpec(memory_space=pltpu.VMEM)
    smem = pl.BlockSpec(memory_space=pltpu.SMEM)
    return pl.pallas_call(
        functools.partial(attention_body, k_raw.shape[1] // hd, cache_rows),
        out_shape=jax.ShapeDtypeStruct((tok_count, q_raw.shape[1] + tag.shape[1]), bf16),
        in_specs=[smem, smem] + [vmem] * 9,
        out_specs=vmem,
    )(lengths, cont_owner, q_raw, k_raw, v_raw, q_gain[None], k_gain[None], cosine, sine, kv_block, tag)


def per_device(
    q_raw,
    k_raw,
    v_raw,
    q_gain,
    k_gain,
    caches,
    lengths,
    cont_owner,
    out_weight,
    residual,
    moe_gain,
    routes,
    gate_weights,
    w_in,
    w_down,
):
    n_groups = lax.axis_size("grp")
    n_columns = lax.axis_size("ep")
    tok_count, model_width = residual.shape
    heads_width = q_raw.shape[1]
    cache_rows = caches.shape[1]
    top_count = routes.shape[1]
    pieces = 4
    cores = 2
    ring_columns = 8
    half = model_width // cores
    expert_count = n_groups * n_columns // pieces
    local = expert_count // n_groups
    capacity = 2
    group_slots = local * capacity
    per_source = n_groups * capacity
    core = lax.axis_index("grp") % cores
    live_rows = jnp.arange(tok_count, dtype=jnp.int32) < lengths[0, 0]

    trades = []
    for g in range(n_groups):
        for p in range(n_columns):
            to = (g - g % 2 + p % 2) * n_columns + p - p % 2 + g % 2
            trades.append((g * n_columns + p, to))
    swap = [(g, g ^ 1) for g in range(n_groups)]

    flat_route = jnp.where(live_rows[:, None], routes, -1).reshape(-1)
    assign_idx = jnp.arange(flat_route.shape[0], dtype=jnp.int32)
    matches = (flat_route[:, None] == flat_route[None, :]) & (assign_idx[None, :] < assign_idx[:, None])
    slot_rank = jnp.sum(matches.astype(jnp.int32), axis=1)
    place = jnp.where(flat_route >= 0, flat_route * capacity + slot_rank, -1)
    slots = jnp.arange(expert_count * capacity, dtype=jnp.int32)
    placed = place.reshape(tok_count, top_count, 1) == slots
    weighted = jnp.sum(jnp.where(placed, gate_weights[:, :, None], 0.0), axis=1)
    chosen = jnp.any(placed, axis=1)
    holder = jnp.sum(
        jnp.where(chosen, jnp.arange(1, tok_count + 1, dtype=jnp.int32)[:, None], 0), axis=0
    ) - 1
    tag = jnp.pad(holder.reshape(n_groups, group_slots).astype(bf16), ((0, 0), (0, 128 - group_slots)))

    kv_block = column_gather(caches.reshape(cache_rows, -1), ring_columns, n_columns)
    kv_block, w_in, w_down = lax.optimization_barrier((kv_block, w_in, w_down))
    w_in = lax.ppermute(w_in, ("grp", "ep"), trades)
    w_down = lax.ppermute(w_down, ("grp", "ep"), trades)
    attended = attention(q_raw, k_raw, v_raw, q_gain, k_gain, kv_block, tag, lengths, cont_owner, cache_rows)
    gathered = group_gather(attended)
    projected = jnp.dot(gathered[:, :heads_width], out_weight, preferred_element_type=f32).astype(bf16)
    attn_proj = exchange(projected.reshape(n_groups, tok_count, -1), "grp", cores, 3)
    attn_proj = attn_proj.transpose(1, 0, 2).reshape(tok_count, model_width)
    hidden_state = (residual.astype(f32) + attn_proj.astype(f32)).astype(bf16)
    moe_in = normed(hidden_state.astype(f32), moe_gain).astype(bf16)

    holders = gathered[:, heads_width : heads_width + group_slots].astype(jnp.int32)
    holders = holders.reshape(n_groups, n_groups, group_slots)
    mine = lax.dynamic_slice_in_dim(holders, lax.axis_index("grp") - core, cores, 1)
    mine = mine.reshape(n_groups, cores, local, capacity).transpose(2, 1, 0, 3)
    source_row = (jnp.arange(n_groups, dtype=jnp.int32) * tok_count)[:, None]
    wanted = jnp.where(mine >= 0, mine + source_row, -1)
    wanted = jnp.broadcast_to(wanted[:, None], (local, pieces // cores) + wanted.shape[1:]).reshape(-1)
    select = (wanted[:, None] == jnp.arange(n_groups * tok_count, dtype=jnp.int32)[None, :]).astype(bf16)

    moe_in, w_in, w_down = lax.optimization_barrier((moe_in, w_in, w_down))
    own_at, other_at = core * half, (1 - core) * half
    w_in_own = lax.dynamic_slice_in_dim(w_in, own_at, half, 1)
    w_in_other = lax.dynamic_slice_in_dim(w_in, other_at, half, 1)
    w_down_own = lax.dynamic_slice_in_dim(w_down, own_at, half, 1)
    w_down_other = lax.dynamic_slice_in_dim(w_down, other_at, half, 1)
    outgoing = jnp.dot(select, half_gather(moe_in), preferred_element_type=f32).astype(bf16)
    received = exchange(outgoing.reshape(n_columns, per_source, half), "ep", ring_columns, 4).reshape(-1, half)
    partner = lax.ppermute(received, "grp", swap)

    def project(which):
        return jnp.dot(received, w_in_own[which], preferred_element_type=f32) + jnp.dot(
            partner, w_in_other[which], preferred_element_type=f32
        )

    inner_act = (jax.nn.silu(project(0)) * project(1)).astype(bf16)
    for_partner = jnp.dot(inner_act, w_down_other, preferred_element_type=f32).astype(bf16)
    from_partner = lax.ppermute(for_partner, "grp", swap)
    partial_out = jnp.dot(inner_act, w_down_own, preferred_element_type=f32)
    partial_out = (partial_out + from_partner.astype(f32)).astype(bf16)
    returned = exchange(partial_out.reshape(n_columns, per_source, half), "ep", ring_columns, 4).reshape(-1, half)
    in_row = jnp.arange(n_columns * per_source, dtype=jnp.int32)
    in_slot, in_column = in_row % per_source, in_row // per_source
    target = (
        in_slot // capacity * (cores * group_slots)
        + in_column % cores * group_slots
        + in_column // pieces * capacity
        + in_slot % capacity
    )
    out_row = jnp.arange(n_groups * cores * group_slots, dtype=jnp.int32)
    gather_sum = (out_row[:, None] == target[None, :]).astype(bf16)
    summed = jnp.dot(gather_sum, returned, preferred_element_type=f32).astype(bf16)
    expert_out = lax.all_to_all(
        summed.reshape(n_groups, cores * group_slots, half), "grp", split_axis=0, concat_axis=0, tiled=True
    )
    expert_out = expert_out.reshape(n_groups // cores, cores, cores * group_slots, half).astype(f32)
    moe_out = jnp.concatenate(
        [
            jnp.dot(weighted, expert_out[:, c].reshape(-1, half), precision=lax.Precision.HIGHEST)
            for c in range(cores)
        ],
        axis=1,
    )
    mixed = jnp.where(live_rows[:, None], hidden_state.astype(f32) + moe_out, 0.0)
    return mixed.astype(bf16)


def solution(mesh):
    in_specs = (
        P(("grp", "ep"), None),
        P(("grp", "ep"), None),
        P(("grp", "ep"), None),
        P(),
        P(),
        P("grp", "ep", None, None, None),
        P("grp", "ep"),
        P("grp", "ep"),
        P(None, "grp"),
        P(("grp", "ep"), None),
        P(),
        P(("grp", "ep"), None),
        P(("grp", "ep"), None),
        P(None, None, ("grp", "ep")),
        P(("grp", "ep"), None),
    )
    out_specs = P(("grp", "ep"), None)
    return jax.shard_map(
        per_device, mesh=mesh, in_specs=in_specs, out_specs=out_specs, check_vma=False
    )
```

```python
import functools
import math

import jax
import jax.numpy as jnp
from jax import lax
from jax.experimental import pallas as pl
from jax.experimental.pallas import tpu as pltpu
from jax.sharding import PartitionSpec as P

theta_base = 1000000.0
eps_norm = 1e-06
f32 = jnp.float32
bf16 = jnp.bfloat16


def normed(values, scales):
    return values * lax.rsqrt(jnp.mean(values * values, axis=-1, keepdims=True) + eps_norm) * scales


def rotation_tables(position, head_width):
    half_width = head_width // 2
    inv_freq = jnp.power(theta_base, -2.0 * jnp.arange(half_width, dtype=f32) / head_width)
    angles = position[:, None] * inv_freq[None, :]
    cosine, sine = jnp.cos(angles), jnp.sin(angles)
    return jnp.concatenate([cosine, cosine], -1), jnp.concatenate([-sine, sine], -1)


MESH = pl.DeviceIdType.MESH


class Flights:
    def __init__(self, send_sems, recv_sems):
        self.sems = send_sems, recv_sems
        self.copies = []

    def send(self, src, dst, device):
        at = len(self.copies)
        copy = pltpu.make_async_remote_copy(
            src, dst, self.sems[0].at[at], self.sems[1].at[at], device_id=device, device_id_type=MESH
        )
        copy.start()
        self.copies.append(copy)
        return copy

    def finish(self):
        for copy in self.copies:
            copy.wait_send()


def greet(devices):
    barrier = pltpu.get_barrier_semaphore()
    for device in devices:
        pl.semaphore_signal(barrier, inc=1, device_id=device, device_id_type=MESH)
    pl.semaphore_wait(barrier, len(devices))


def ring_order(n):
    order = [0]
    for step in range(1, n // 2 + 1):
        order.append(-step)
        if step < n - n // 2:
            order.append(step)
    return order


def column_gather_body(columns, in_ref, out_ref, local_sem, send_sems, recv_sems):
    g, p = lax.axis_index("grp"), lax.axis_index("ep")
    n_x = lax.axis_size("ep") // columns
    x, y = p // columns, p % columns
    half = in_ref.shape[0] // 2
    up = (g, x * columns + (y + 1) % columns)
    down = (g, x * columns + (y + columns - 1) % columns)
    right = (g, (x + 1) % n_x * columns + y)
    left = (g, (x + n_x - 1) % n_x * columns + y)
    greet([up, down, right, left])
    flights = Flights(send_sems, recv_sems)
    local = pltpu.make_async_copy(in_ref, out_ref.at[p], local_sem)
    local.start()

    def block(across, along):
        return (x + across + n_x) % n_x * columns + (y + along + columns) % columns

    coming, sideways = {}, []
    order = ring_order(columns)
    for along in order:
        here = out_ref.at[block(0, along)]
        if along == 0:
            source = in_ref
        else:
            coming[along].wait_recv()
            source = here
        if along <= 0 and along - 1 in order:
            coming[along - 1] = flights.send(source, here, up)
        if along >= 0 and along + 1 in order:
            coming[along + 1] = flights.send(source, here, down)
        sideways.append((flights.send(source, here, right), flights.send(source, here, left)))
    last = []
    for along, (from_left, from_right) in zip(order, sideways):
        from_left.wait_recv()
        part = out_ref.at[block(-1, along), pl.ds(0, half)]
        last.append(flights.send(part, part, right))
        from_right.wait_recv()
        part = out_ref.at[block(1, along), pl.ds(half, half)]
        last.append(flights.send(part, part, left))
    for copy in last:
        copy.wait_recv()
    local.wait()
    flights.finish()


def column_gather(rows, columns, n_columns):
    count = columns - 1 + 4 * columns
    vmem = pl.BlockSpec(memory_space=pltpu.VMEM)
    gathered = pl.pallas_call(
        functools.partial(column_gather_body, columns),
        out_shape=jax.ShapeDtypeStruct((n_columns,) + rows.shape, rows.dtype),
        in_specs=[vmem],
        out_specs=vmem,
        scratch_shapes=[
            pltpu.SemaphoreType.DMA,
            pltpu.SemaphoreType.DMA((count,)),
            pltpu.SemaphoreType.DMA((count,)),
        ],
        compiler_params=pltpu.CompilerParams(collective_id=0, has_side_effects=True),
        cost_estimate=pl.CostEstimate(flops=10**9, bytes_accessed=1 << 27, transcendentals=0),
    )(rows)
    return gathered.reshape(-1, rows.shape[1])


def group_places():
    g, p = lax.axis_index("grp"), lax.axis_index("ep")
    depth = lax.axis_size("grp") // 2
    z, core = g // 2, g % 2
    up = ((z + 1) % depth * 2 + core, p)
    down = ((z + depth - 1) % depth * 2 + core, p)
    partner = (z * 2 + 1 - core, p)
    return g, depth, z, core, up, down, partner


def group_gather_body(in_ref, out_ref, local_sem, send_sems, recv_sems):
    g, depth, z, core, up, down, partner = group_places()
    greet([up, down, partner])
    flights = Flights(send_sems, recv_sems)
    local = pltpu.make_async_copy(in_ref, out_ref.at[g], local_sem)
    local.start()
    coming, handed = {}, []
    order = ring_order(depth)
    lanes = 128
    width = in_ref.shape[1]
    middle = width // lanes // 2 * lanes
    chunks = [pl.ds(0, middle), pl.ds(middle, width - middle)]
    for along in order:
        for c, chunk in enumerate(chunks):
            here = out_ref.at[(z + along + depth) % depth * 2 + core, :, chunk]
            if along == 0:
                source = in_ref.at[:, chunk]
            else:
                coming[along, c].wait_recv()
                source = here
            if along <= 0 and along - 1 in order:
                coming[along - 1, c] = flights.send(source, here, up)
            if along >= 0 and along + 1 in order:
                coming[along + 1, c] = flights.send(source, here, down)
            handed.append(flights.send(source, here, partner))
    for copy in handed:
        copy.wait_recv()
    local.wait()
    flights.finish()


def half_gather_body(in_ref, out_ref, local_sem, send_sems, recv_sems):
    g, depth, z, core, up, down, partner = group_places()
    half = out_ref.shape[2]
    greet([up, down, partner])
    flights = Flights(send_sems, recv_sems)
    own = in_ref.at[:, pl.ds(pl.multiple_of(core * half, half), half)]
    other = in_ref.at[:, pl.ds(pl.multiple_of((1 - core) * half, half), half)]
    swapped = flights.send(other, out_ref.at[g], partner)
    local = pltpu.make_async_copy(own, out_ref.at[g], local_sem)
    local.start()
    swapped.wait_recv()
    local.wait()
    coming = {}
    order = ring_order(depth)
    for along in order:
        here = out_ref.at[pl.ds((z + along + depth) % depth * 2, 2)]
        if along != 0:
            coming[along].wait_recv()
        if along <= 0 and along - 1 in order:
            coming[along - 1] = flights.send(here, here, up)
        if along >= 0 and along + 1 in order:
            coming[along + 1] = flights.send(here, here, down)
    flights.finish()


def over_groups(body, count, width, collective_id, rows):
    n_groups = lax.axis_size("grp")
    vmem = pl.BlockSpec(memory_space=pltpu.VMEM)
    gathered = pl.pallas_call(
        body,
        out_shape=jax.ShapeDtypeStruct((n_groups, rows.shape[0], width), rows.dtype),
        in_specs=[vmem],
        out_specs=vmem,
        scratch_shapes=[
            pltpu.SemaphoreType.DMA,
            pltpu.SemaphoreType.DMA((count,)),
            pltpu.SemaphoreType.DMA((count,)),
        ],
        compiler_params=pltpu.CompilerParams(collective_id=collective_id, has_side_effects=True),
    )(rows)
    return gathered.reshape(-1, width)


def group_gather(rows):
    return over_groups(group_gather_body, 2 * (lax.axis_size("grp") - 1), rows.shape[1], 1, rows)


def half_gather(rows):
    return over_groups(half_gather_body, lax.axis_size("grp") // 2, rows.shape[1] // 2, 2, rows)


def exchange_body(axis, inner, in_ref, out_ref, local_sem, send_sems, recv_sems):
    g, p = lax.axis_index("grp"), lax.axis_index("ep")
    me = lax.axis_index(axis)
    outer = lax.axis_size(axis) // inner
    far = lambda n: sorted(range(n), key=lambda d: (-min(d, n - d), d))
    steps = [(a, b) for b in far(inner) for a in far(outer) if (a, b) != (0, 0)]

    def place(a, b):
        return (me // inner + a) % outer * inner + (me % inner + b) % inner

    peers = [place(a, b) for a, b in steps]
    device = (lambda i: (i, p)) if axis == "grp" else (lambda i: (g, i))
    greet([device(i) for i in peers])
    flights = Flights(send_sems, recv_sems)
    copies = [flights.send(in_ref.at[i], out_ref.at[me], device(i)) for i in peers]
    local = pltpu.make_async_copy(in_ref.at[me], out_ref.at[me], local_sem)
    local.start()
    for copy in copies:
        copy.wait_recv()
    local.wait()
    flights.finish()


def exchange(blocks, axis, inner, collective_id):
    count = blocks.shape[0] - 1
    vmem = pl.BlockSpec(memory_space=pltpu.VMEM)
    return pl.pallas_call(
        functools.partial(exchange_body, axis, inner),
        out_shape=jax.ShapeDtypeStruct(blocks.shape, blocks.dtype),
        in_specs=[vmem],
        out_specs=vmem,
        scratch_shapes=[
            pltpu.SemaphoreType.DMA,
            pltpu.SemaphoreType.DMA((count,)),
            pltpu.SemaphoreType.DMA((count,)),
        ],
        compiler_params=pltpu.CompilerParams(collective_id=collective_id, has_side_effects=True),
    )(blocks)


def attention_body(
    kv_heads, cache_rows, len_ref, own_ref, q_ref, k_ref, v_ref, qg_ref, kg_ref, cos_ref, sin_ref, kv_ref, tag_ref, out_ref
):
    tok_count = q_ref.shape[0]
    hd = qg_ref.shape[1]
    width = kv_heads * hd
    group = q_ref.shape[1] // width
    rows = group * tok_count
    scaling = 1.0 / math.sqrt(hd)
    seq_len = len_ref[0, 0]
    start = pl.multiple_of(own_ref[0, 0] * cache_rows, cache_rows)
    cosine, sine = cos_ref[...], sin_ref[...]

    def prepared(raw, gain):
        values = normed(raw.astype(f32), gain)
        return (values * cosine + pltpu.roll(values, hd // 2, 1) * sine).astype(bf16)

    slot = lax.broadcasted_iota(jnp.int32, (rows, tok_count), 0) % tok_count
    other = lax.broadcasted_iota(jnp.int32, (rows, tok_count), 1)
    causal = (other <= slot) & (other < seq_len)
    live = lax.broadcasted_iota(jnp.int32, (rows, hd), 0) % tok_count < seq_len
    contract = (((1,), (1,)), ((), ()))

    def weighed(queries, keys):
        return jnp.exp(lax.dot_general(queries, keys, contract, preferred_element_type=f32) * scaling)

    out_ref[:, pl.ds(q_ref.shape[1], tag_ref.shape[1])] = tag_ref[...]
    for h in range(kv_heads):
        span = pl.ds(h * hd, hd)
        queries = jnp.concatenate(
            [prepared(q_ref[:, pl.ds((h * group + j) * hd, hd)], qg_ref[...]) for j in range(group)], 0
        )
        pre = weighed(queries, kv_ref[:, span])
        cont = weighed(queries, kv_ref[pl.ds(start, cache_rows), pl.ds(2 * width + h * hd, hd)])
        own = jnp.where(causal, weighed(queries, prepared(k_ref[:, span], kg_ref[...])), 0.0)
        numerator = (
            jnp.dot(pre.astype(bf16), kv_ref[:, pl.ds(width + h * hd, hd)], preferred_element_type=f32)
            + jnp.dot(
                cont.astype(bf16),
                kv_ref[pl.ds(start, cache_rows), pl.ds(3 * width + h * hd, hd)],
                preferred_element_type=f32,
            )
            + jnp.dot(own.astype(bf16), v_ref[:, span], preferred_element_type=f32)
        )
        denominator = (
            jnp.sum(pre, 1, keepdims=True) + jnp.sum(cont, 1, keepdims=True) + jnp.sum(own, 1, keepdims=True)
        )
        result = jnp.where(live, numerator / denominator, 0.0).astype(bf16)
        for j in range(group):
            out_ref[:, pl.ds((h * group + j) * hd, hd)] = result[j * tok_count : (j + 1) * tok_count]


def attention(q_raw, k_raw, v_raw, q_gain, k_gain, kv_block, tag, lengths, cont_owner, cache_rows):
    hd = q_gain.shape[0]
    tok_count = q_raw.shape[0]
    position = (kv_block.shape[0] + cache_rows + jnp.arange(tok_count, dtype=jnp.int32)).astype(f32)
    cosine, sine = rotation_tables(position, hd)
    vmem = pl.BlockSpec(memory_space=pltpu.VMEM)
    smem = pl.BlockSpec(memory_space=pltpu.SMEM)
    return pl.pallas_call(
        functools.partial(attention_body, k_raw.shape[1] // hd, cache_rows),
        out_shape=jax.ShapeDtypeStruct((tok_count, q_raw.shape[1] + tag.shape[1]), bf16),
        in_specs=[smem, smem] + [vmem] * 9,
        out_specs=vmem,
    )(lengths, cont_owner, q_raw, k_raw, v_raw, q_gain[None], k_gain[None], cosine, sine, kv_block, tag)


def per_device(
    q_raw,
    k_raw,
    v_raw,
    q_gain,
    k_gain,
    caches,
    lengths,
    cont_owner,
    out_weight,
    residual,
    moe_gain,
    routes,
    gate_weights,
    w_in,
    w_down,
):
    n_groups = lax.axis_size("grp")
    n_columns = lax.axis_size("ep")
    tok_count, model_width = residual.shape
    heads_width = q_raw.shape[1]
    cache_rows = caches.shape[1]
    top_count = routes.shape[1]
    pieces = 4
    cores = 2
    ring_columns = 8
    half = model_width // cores
    expert_count = n_groups * n_columns // pieces
    local = expert_count // n_groups
    capacity = 2
    group_slots = local * capacity
    per_source = n_groups * capacity
    core = lax.axis_index("grp") % cores
    live_rows = jnp.arange(tok_count, dtype=jnp.int32) < lengths[0, 0]

    trades = []
    for g in range(n_groups):
        for p in range(n_columns):
            to = (g - g % 2 + p % 2) * n_columns + p - p % 2 + g % 2
            trades.append((g * n_columns + p, to))
    swap = [(g, g ^ 1) for g in range(n_groups)]

    flat_route = jnp.where(live_rows[:, None], routes, -1).reshape(-1)
    assign_idx = jnp.arange(flat_route.shape[0], dtype=jnp.int32)
    matches = (flat_route[:, None] == flat_route[None, :]) & (assign_idx[None, :] < assign_idx[:, None])
    slot_rank = jnp.sum(matches.astype(jnp.int32), axis=1)
    place = jnp.where(flat_route >= 0, flat_route * capacity + slot_rank, -1)
    slots = jnp.arange(expert_count * capacity, dtype=jnp.int32)
    placed = place.reshape(tok_count, top_count, 1) == slots
    weighted = jnp.sum(jnp.where(placed, gate_weights[:, :, None], 0.0), axis=1)
    chosen = jnp.any(placed, axis=1)
    holder = jnp.sum(
        jnp.where(chosen, jnp.arange(1, tok_count + 1, dtype=jnp.int32)[:, None], 0), axis=0
    ) - 1
    tag = jnp.pad(holder.reshape(n_groups, group_slots).astype(bf16), ((0, 0), (0, 128 - group_slots)))

    kv_block = column_gather(caches.reshape(cache_rows, -1), ring_columns, n_columns)
    kv_block, w_in, w_down = lax.optimization_barrier((kv_block, w_in, w_down))
    w_in = lax.ppermute(w_in, ("grp", "ep"), trades)
    w_down = lax.ppermute(w_down, ("grp", "ep"), trades)
    attended = attention(q_raw, k_raw, v_raw, q_gain, k_gain, kv_block, tag, lengths, cont_owner, cache_rows)
    gathered = group_gather(attended)
    projected = jnp.dot(gathered[:, :heads_width], out_weight, preferred_element_type=f32).astype(bf16)
    attn_proj = exchange(projected.reshape(n_groups, tok_count, -1), "grp", cores, 3)
    attn_proj = attn_proj.transpose(1, 0, 2).reshape(tok_count, model_width)
    hidden_state = (residual.astype(f32) + attn_proj.astype(f32)).astype(bf16)
    moe_in = normed(hidden_state.astype(f32), moe_gain).astype(bf16)

    holders = gathered[:, heads_width : heads_width + group_slots].astype(jnp.int32)
    holders = holders.reshape(n_groups, n_groups, group_slots)
    mine = lax.dynamic_slice_in_dim(holders, lax.axis_index("grp") - core, cores, 1)
    mine = mine.reshape(n_groups, cores, local, capacity).transpose(2, 1, 0, 3)
    source_row = (jnp.arange(n_groups, dtype=jnp.int32) * tok_count)[:, None]
    wanted = jnp.where(mine >= 0, mine + source_row, -1)
    wanted = jnp.broadcast_to(wanted[:, None], (local, pieces // cores) + wanted.shape[1:]).reshape(-1)
    select = (wanted[:, None] == jnp.arange(n_groups * tok_count, dtype=jnp.int32)[None, :]).astype(bf16)

    moe_in, w_in, w_down = lax.optimization_barrier((moe_in, w_in, w_down))
    own_at, other_at = core * half, (1 - core) * half
    w_in_own = lax.dynamic_slice_in_dim(w_in, own_at, half, 1)
    w_in_other = lax.dynamic_slice_in_dim(w_in, other_at, half, 1)
    w_down_own = lax.dynamic_slice_in_dim(w_down, own_at, half, 1)
    w_down_other = lax.dynamic_slice_in_dim(w_down, other_at, half, 1)
    outgoing = jnp.dot(select, half_gather(moe_in), preferred_element_type=f32).astype(bf16)
    received = exchange(outgoing.reshape(n_columns, per_source, half), "ep", ring_columns, 4).reshape(-1, half)
    partner = lax.ppermute(received, "grp", swap)

    def project(which):
        return jnp.dot(received, w_in_own[which], preferred_element_type=f32) + jnp.dot(
            partner, w_in_other[which], preferred_element_type=f32
        )

    inner_act = (jax.nn.silu(project(0)) * project(1)).astype(bf16)
    for_partner = jnp.dot(inner_act, w_down_other, preferred_element_type=f32).astype(bf16)
    from_partner = lax.ppermute(for_partner, "grp", swap)
    partial_out = jnp.dot(inner_act, w_down_own, preferred_element_type=f32)
    partial_out = (partial_out + from_partner.astype(f32)).astype(bf16)
    returned = lax.all_to_all(
        partial_out.reshape(n_columns, per_source, half), "ep", split_axis=0, concat_axis=0, tiled=True
    ).reshape(-1, half)
    in_row = jnp.arange(n_columns * per_source, dtype=jnp.int32)
    in_slot, in_column = in_row % per_source, in_row // per_source
    target = (
        in_slot // capacity * (cores * group_slots)
        + in_column % cores * group_slots
        + in_column // pieces * capacity
        + in_slot % capacity
    )
    out_row = jnp.arange(n_groups * cores * group_slots, dtype=jnp.int32)
    gather_sum = (out_row[:, None] == target[None, :]).astype(bf16)
    summed = jnp.dot(gather_sum, returned, preferred_element_type=f32).astype(bf16)
    expert_out = lax.all_to_all(
        summed.reshape(n_groups, cores * group_slots, half), "grp", split_axis=0, concat_axis=0, tiled=True
    )
    expert_out = expert_out.reshape(n_groups // cores, cores, cores * group_slots, half).astype(f32)
    moe_out = jnp.concatenate(
        [
            jnp.dot(weighted, expert_out[:, c].reshape(-1, half), precision=lax.Precision.HIGHEST)
            for c in range(cores)
        ],
        axis=1,
    )
    mixed = jnp.where(live_rows[:, None], hidden_state.astype(f32) + moe_out, 0.0)
    return mixed.astype(bf16)


def solution(mesh):
    in_specs = (
        P(("grp", "ep"), None),
        P(("grp", "ep"), None),
        P(("grp", "ep"), None),
        P(),
        P(),
        P("grp", "ep", None, None, None),
        P("grp", "ep"),
        P("grp", "ep"),
        P(None, "grp"),
        P(("grp", "ep"), None),
        P(),
        P(("grp", "ep"), None),
        P(("grp", "ep"), None),
        P(None, None, ("grp", "ep")),
        P(("grp", "ep"), None),
    )
    out_specs = P(("grp", "ep"), None)
    return jax.shard_map(
        per_device, mesh=mesh, in_specs=in_specs, out_specs=out_specs, check_vma=False
    )
```
